512 devices in a mesh: slab: 32 (over x, y, z_hi), tile: 16 (over z_lo, core).
Axes of the slice: x: 4, y: 4, z: 16 (z_hi: 2, z_lo: 8; z = z_hi * 8 + z_lo), core: 2. Of those that a mesh axis runs over, the one named last changes fastest.
Arguments:
- field: float32 [256, 256, 1024], P('slab', 'tile'), may hold values from -1 to 1
- dual: float32 [3, 256, 256, 1024], P(None, 'slab', 'tile'), may hold values from -0.5 to 0.5
- depth: float32 [32, 2, 4, 256, 1024], P('slab', None, None, 'tile'), may hold values from 0 to 256
- owner: int32 [2], replicated, may hold values from 0 to 31
- visible: int32 [2, 4, 16], P(None, None, 'tile'), may hold values 0 or 1
Outputs:
- field_out: float32 [256, 256, 1024], P('slab', 'tile')
- dual_out: float32 [3, 256, 256, 1024], P(None, 'slab', 'tile')
The draws below stay inside these ranges and needn't reach their ends.
All inputs are finite; a program needn't handle non-finite values. No bound on the sum of `visible` on one device may be relied on, other than what follows from the above.
Results may differ from the reference program's by a relative error of at most 0.00002.
Values sent between devices are 32-bit elements; how exact they have to be, the bound alone decides.
No kernel may reach another device: no remote copies, remote signals or barrier semaphores. Data moves between devices by JAX's collectives and lax.ppermute only.
A program may use at most 64 MiB of HBM per device.

```python
import jax
import jax.numpy as jnp

CX = 16
NY = 1024
VIEWS = 4
BINS = 8
BAND = 6
ITERS = 2
NZ = 256
NX = 256
N_SLAB = 32
N_TILE = 16


def touch_ends(array, key, low, largest):
    shape = array.shape
    spot = [jax.random.randint(jax.random.fold_in(key, axis), (), 0, shape[axis]) for axis in range(len(shape))]
    array = array.at[tuple(spot)].set(low)
    longest = shape.index(max(shape))
    spot[longest] = (spot[longest] + 1) % shape[longest]
    return array.at[tuple(spot)].set(largest)


def block_scale(own_key, dims, pieces, least, top_value):
    gain = 1.0
    for position, parts in pieces:
        draws = jax.random.uniform(jax.random.fold_in(jax.random.fold_in(own_key, 6), position), (parts,), jnp.float32, least / len(pieces), top_value / len(pieces))
        gain = gain * jnp.repeat(jnp.exp(draws), dims[position] // parts).reshape((-1,) + (1,) * (len(dims) - 1 - position))
    return gain


def setup_inputs(seed: int = 0) -> dict:
    key_list = jax.random.split(jax.random.key(seed), 6)
    field = jnp.clip(jax.random.uniform(key_list[0], (NZ, NX, NY), jnp.float32, -1.0, 1.0) * block_scale(key_list[0], (NZ, NX, NY), ((0, 32), (1, 16)), -0.4, 0.0), -1.0, 1.0)
    dual = jnp.clip(jax.random.uniform(key_list[1], (3, NZ, NX, NY), jnp.float32, -0.5, 0.5) * block_scale(key_list[1], (3, NZ, NX, NY), ((1, 32), (2, 16)), -0.4, 0.0), -0.5, 0.5)
    depth = jnp.clip(256.0 * jax.random.uniform(key_list[2], (N_SLAB, ITERS, VIEWS, NX, NY), jnp.float32) ** block_scale(key_list[2], (N_SLAB, ITERS, VIEWS, NX, NY), ((0, 32), (3, 16)), -0.2, 0.2), 0.0, 256.0)
    owner = jax.random.randint(key_list[3], (ITERS,), 0, N_SLAB).astype(jnp.int32)
    visible = touch_ends((jax.random.randint(key_list[4], (ITERS, VIEWS, N_TILE), 0, 4) < 3).astype(jnp.int32), jax.random.fold_in(key_list[4], 1), 0, 1)
    return dict(field=field, dual=dual, depth=depth, owner=owner, visible=visible)


def add_votes(histogram, depth_map, seen, zpos):
    ratio = (depth_map[None, :, :] - zpos) / float(BAND)
    weight = jnp.clip(ratio + 2.0, 0.0, 1.0) * seen
    place = (jnp.clip(ratio, -1.0, 1.0) + 1.0) * ((BINS - 1) / 2.0)
    return [histogram[bin_index] + weight * jnp.maximum(0.0, 1.0 - jnp.abs(place - float(bin_index))) for bin_index in range(BINS)]

def proximal(values, histogram):
    total = histogram[0]
    for bin_index in range(1, BINS):
        total = total + histogram[bin_index]
    weights = -total
    best = jnp.minimum(values - 0.05 * weights, -1.0)
    weights = weights + 2.0 * histogram[0]
    for bin_index in range(1, BINS):
        centre = -1.0 + 2.0 * bin_index / (BINS - 1)
        best = jnp.maximum(best, jnp.minimum(values - 0.05 * weights, centre))
        weights = weights + 2.0 * histogram[bin_index]
    return jnp.maximum(best, values - 0.05 * weights)

def reference(field, dual, depth, owner, visible):
    zpos = jnp.arange(NZ, dtype=jnp.int32)[:, None, None]
    xpos = jnp.arange(NX, dtype=jnp.int32)[None, :, None]
    ypos = jnp.arange(NY, dtype=jnp.int32)[None, None, :]
    zfloat = zpos.astype(jnp.float32)
    strip = jnp.arange(NX, dtype=jnp.int32) // CX
    histogram = [jnp.zeros((NZ, NX, NY), jnp.float32) for bin_index in range(BINS)]
    current = field
    dual_z, dual_x, dual_y = (dual[0], dual[1], dual[2])
    extra = field
    for step_index in range(ITERS):
        for view_index in range(VIEWS):
            depth_map = depth[owner[step_index], step_index, view_index]
            seen = visible[step_index, view_index][strip].astype(jnp.float32)[None, :, None]
            histogram = add_votes(histogram, depth_map, seen, zfloat)
        zero_z = jnp.zeros((1, NX, NY), jnp.float32)
        zero_x = jnp.zeros((NZ, 1, NY), jnp.float32)
        zero_y = jnp.zeros((NZ, NX, 1), jnp.float32)
        grad_z = jnp.where(zpos < NZ - 1, jnp.concatenate([extra[1:], zero_z], 0) - extra, 0.0)
        grad_x = jnp.where(xpos < NX - 1, jnp.concatenate([extra[:, 1:], zero_x], 1) - extra, 0.0)
        grad_y = jnp.where(ypos < NY - 1, jnp.concatenate([extra[:, :, 1:], zero_y], 2) - extra, 0.0)
        moved_z = dual_z + 0.25 * grad_z
        moved_x = dual_x + 0.25 * grad_x
        moved_y = dual_y + 0.25 * grad_y
        scale = jnp.maximum(1.0, jnp.sqrt(moved_z * moved_z + moved_x * moved_x + moved_y * moved_y))
        dual_z = jnp.where(zpos < NZ - 1, moved_z / scale, 0.0)
        dual_x = jnp.where(xpos < NX - 1, moved_x / scale, 0.0)
        dual_y = jnp.where(ypos < NY - 1, moved_y / scale, 0.0)
        prev_z = jnp.concatenate([zero_z, dual_z[:-1]], 0)
        prev_x = jnp.concatenate([zero_x, dual_x[:, :-1]], 1)
        prev_y = jnp.concatenate([zero_y, dual_y[:, :, :-1]], 2)
        divergence = dual_z - prev_z + (dual_x - prev_x) + (dual_y - prev_y)
        updated = proximal(current + 0.25 * divergence, histogram)
        extra = 2.0 * updated - current
        current = updated
    return (current, jnp.stack([dual_z, dual_x, dual_y]))
```

```python
import jax
import jax.numpy as jnp
from jax import lax
from jax.sharding import PartitionSpec as P

VIEWS = 4
BINS = 8
BAND = 6
ITERS = 2


def from_roots(batches, roots):
    groups = [[2 * place + half for place in range(16)] for half in range(2)]
    flip = [(index, index ^ 1) for index in range(32)]
    my_half = lax.axis_index("slab") % 2
    pieces = batches.reshape(ITERS, VIEWS, 2, 8, 2, 4, 128).transpose(1, 2, 4, 0, 5, 3, 6)
    pieces = pieces.reshape(16, ITERS, 4, 8, 128)
    spread = lax.all_to_all(pieces, "slab", 0, 0, axis_index_groups=groups)
    kept = jnp.stack([
        lax.dynamic_index_in_dim(spread[:, step], roots[step] // 2, 0, keepdims=False) for step in range(ITERS)
    ])
    across = lax.ppermute(kept, "slab", flip)
    right_half = (roots % 2 == my_half)[:, None, None, None]
    kept = jnp.where(right_half, kept, across)
    whole = lax.all_to_all(
        jnp.broadcast_to(kept[None], (16,) + kept.shape), "slab", 0, 0, axis_index_groups=groups
    )
    whole = whole.reshape(VIEWS, 2, 2, ITERS, 4, 8, 128).transpose(3, 0, 1, 5, 2, 4, 6)
    return whole.reshape(ITERS, VIEWS, 16, 1024)


def passed_along(value, axis, steps):
    count = lax.axis_size(axis)
    first, last = (max(0, -steps), min(count, count - steps))
    return lax.ppermute(value, axis, [(source, source + steps) for source in range(first, last)])


def add_votes(histogram, depth_map, seen, zfloat):
    ratio = (depth_map[None, :, :] - zfloat) / float(BAND)
    weight = jnp.clip(ratio + 2.0, 0.0, 1.0) * seen
    place = (jnp.clip(ratio, -1.0, 1.0) + 1.0) * ((BINS - 1) / 2.0)
    return [
        histogram[bin_index] + weight * jnp.maximum(0.0, 1.0 - jnp.abs(place - float(bin_index)))
        for bin_index in range(BINS)
    ]


def proximal(values, histogram):
    total = histogram[0]
    for bin_index in range(1, BINS):
        total = total + histogram[bin_index]
    weights = -total
    best = jnp.minimum(values - 0.05 * weights, -1.0)
    weights = weights + 2.0 * histogram[0]
    for bin_index in range(1, BINS):
        centre = -1.0 + 2.0 * bin_index / (BINS - 1)
        best = jnp.maximum(best, jnp.minimum(values - 0.05 * weights, centre))
        weights = weights + 2.0 * histogram[bin_index]
    return jnp.maximum(best, values - 0.05 * weights)


def dual_step(
    dual_z, dual_x, dual_y, here, ahead_z, ahead_x, zpos, xpos, ypos, total_z, total_x, total_y
):
    zero_y = jnp.zeros(here.shape[:2] + (1,), jnp.float32)
    ahead_y = jnp.concatenate([here[:, :, 1:], zero_y], 2)
    grad_z = jnp.where(zpos < total_z - 1, ahead_z - here, 0.0)
    grad_x = jnp.where(xpos < total_x - 1, ahead_x - here, 0.0)
    grad_y = jnp.where(ypos < total_y - 1, ahead_y - here, 0.0)
    moved_z = dual_z + 0.25 * grad_z
    moved_x = dual_x + 0.25 * grad_x
    moved_y = dual_y + 0.25 * grad_y
    scale = jnp.maximum(1.0, jnp.sqrt(moved_z * moved_z + moved_x * moved_x + moved_y * moved_y))
    inside_z = (zpos >= 0) & (zpos < total_z - 1)
    inside_x = (xpos >= 0) & (xpos < total_x - 1)
    new_z = jnp.where(inside_z, moved_z / scale, 0.0)
    new_x = jnp.where(inside_x, moved_x / scale, 0.0)
    new_y = jnp.where(ypos < total_y - 1, moved_y / scale, 0.0)
    return (new_z, new_x, new_y)


def per_device(field, dual, depth, owner, visible):
    slab_cells, strip_cells, depth_cells = field.shape
    total_z = slab_cells * lax.axis_size("slab")
    total_x = strip_cells * lax.axis_size("tile")
    slab_start = lax.axis_index("slab") * slab_cells
    strip_start = lax.axis_index("tile") * strip_cells
    zpos = slab_start + jnp.arange(slab_cells, dtype=jnp.int32)[:, None, None]
    xpos = strip_start + jnp.arange(strip_cells, dtype=jnp.int32)[None, :, None]
    ypos = jnp.arange(depth_cells, dtype=jnp.int32)[None, None, :]
    zfloat = zpos.astype(jnp.float32)
    histogram = [jnp.zeros(field.shape, jnp.float32) for bin_index in range(BINS)]
    current = field
    dual_z, dual_x, dual_y = (dual[0], dual[1], dual[2])
    extra = field
    zero_y = jnp.zeros((slab_cells, strip_cells, 1), jnp.float32)
    batches = from_roots(depth[0], owner)
    for step_index in range(ITERS):
        batch = batches[step_index]
        for view_index in range(VIEWS):
            seen = visible[step_index, view_index, 0].astype(jnp.float32)
            histogram = add_votes(histogram, batch[view_index], seen, zfloat)
        below = passed_along(extra[0:1], "slab", -1)
        beside = passed_along(extra[:, 0:1], "tile", -1)
        ahead_z = jnp.concatenate([extra[1:], below], 0)
        ahead_x = jnp.concatenate([extra[:, 1:], beside], 1)
        dual_z, dual_x, dual_y = dual_step(
            dual_z,
            dual_x,
            dual_y,
            extra,
            ahead_z,
            ahead_x,
            zpos,
            xpos,
            ypos,
            total_z,
            total_x,
            depth_cells,
        )
        above = passed_along(dual_z[-1:], "slab", 1)
        before = passed_along(dual_x[:, -1:], "tile", 1)
        prev_z = jnp.concatenate([above, dual_z[:-1]], 0)
        prev_x = jnp.concatenate([before, dual_x[:, :-1]], 1)
        prev_y = jnp.concatenate([zero_y, dual_y[:, :, :-1]], 2)
        divergence = dual_z - prev_z + (dual_x - prev_x) + (dual_y - prev_y)
        updated = proximal(current + 0.25 * divergence, histogram)
        extra = 2.0 * updated - current
        current = updated
    return (current, jnp.stack([dual_z, dual_x, dual_y]))


def solution(mesh):
    placed = (
        P("slab", "tile", None),
        P(None, "slab", "tile", None),
        P("slab", None, None, "tile", None),
        P(),
        P(None, None, "tile"),
    )
    return jax.shard_map(
        per_device,
        mesh=mesh,
        in_specs=placed,
        out_specs=(P("slab", "tile", None), P(None, "slab", "tile", None)),
        check_vma=False,
    )
```

```python
import jax
import jax.numpy as jnp
from jax import lax
from jax.experimental import pallas as pl
from jax.experimental.pallas import tpu as pltpu
from jax.sharding import PartitionSpec as P

VIEWS = 4
BINS = 8
BAND = 6
ITERS = 2

LAYERS = 8
ROWS = 16
LANES = 1024
STEP = 0.1
Z_LAST = 31
X_LAST = 15


def call(kernel, out_shapes, flops, in_specs=None):
    return pl.pallas_call(
        kernel,
        out_shape=tuple(jax.ShapeDtypeStruct(shape, jnp.float32) for shape in out_shapes),
        in_specs=in_specs,
        compiler_params=pltpu.CompilerParams(vmem_limit_bytes=16 << 20),
        cost_estimate=pl.CostEstimate(flops=flops, transcendentals=0, bytes_accessed=4 << 20),
        name=kernel.__name__ if hasattr(kernel, "__name__") else kernel.func.__name__,
    )


VMEM = pl.BlockSpec(memory_space=pltpu.VMEM)
SMEM = pl.BlockSpec(memory_space=pltpu.SMEM)
ANY = pl.BlockSpec(memory_space=pl.ANY)


def row_ids():
    return lax.broadcasted_iota(jnp.int32, (ROWS, LANES), 0)


def lane_ids():
    return lax.broadcasted_iota(jnp.int32, (ROWS, LANES), 1)


def spread_row(row):
    return jnp.broadcast_to(row, (ROWS, LANES))


def dual_layer(here, ahead_z, ahead_row, dual_z, dual_x, dual_y, z_end):
    row, lane = row_ids(), lane_ids()
    x_end = (row == ROWS - 1) & (lax.axis_index("tile") == X_LAST)
    y_end = lane == LANES - 1
    ahead_x = jnp.where(row == ROWS - 1, spread_row(ahead_row), pltpu.roll(here, ROWS - 1, 0))
    ahead_y = pltpu.roll(here, LANES - 1, 1)
    moved_z = dual_z + 0.25 * jnp.where(z_end, 0.0, ahead_z - here)
    moved_x = dual_x + 0.25 * jnp.where(x_end, 0.0, ahead_x - here)
    moved_y = dual_y + 0.25 * jnp.where(y_end, 0.0, ahead_y - here)
    norm = moved_z * moved_z + moved_x * moved_x + moved_y * moved_y
    scale = 1.0 / jnp.sqrt(jnp.maximum(norm, 1.0))
    return (
        jnp.where(z_end, 0.0, moved_z * scale),
        jnp.where(x_end, 0.0, moved_x * scale),
        jnp.where(y_end, 0.0, moved_y * scale),
    )


def flux(dual_x, dual_y, before_row):
    before = jnp.where(row_ids() == 0, spread_row(before_row), pltpu.roll(dual_x, 1, 0))
    return (dual_x - before) + (dual_y - pltpu.roll(dual_y, 1, 1))


def first_layer(field, dual, ahead, message):
    here = field[0]
    dual_z, dual_x, dual_y = dual_layer(here, field[1], ahead[0:1, :], dual[0, 0], dual[1, 0], dual[2, 0], False)
    message[0:16, :] = here
    message[16:32, :] = here + 0.25 * (dual_z + flux(dual_x, dual_y, jnp.zeros((1, LANES), jnp.float32)))
    message[32:40, :] = dual_x[8:16, :]


def all_duals(field, dual, ahead, below, new_dual, top, side):
    slab_end = lax.axis_index("slab") == Z_LAST
    for layer in range(LAYERS):
        last = layer == LAYERS - 1
        dual_z, dual_x, dual_y = dual_layer(
            field[layer],
            below[0:16, :] if last else field[layer + 1],
            ahead[layer : layer + 1, :],
            dual[0, layer],
            dual[1, layer],
            dual[2, layer],
            slab_end if last else False,
        )
        new_dual[0, layer] = dual_z
        new_dual[1, layer] = dual_x
        new_dual[2, layer] = dual_y
        side[layer : layer + 1, :] = dual_x[15:16, :]
        if last:
            top[...] = dual_z
    side[8:16, :] = jnp.zeros((8, LANES), jnp.float32)
    side[8:9, :] = below[39:40, :]


def all_steps(field, dual, above, before, below, values):
    for layer in range(LAYERS):
        prev = above[...] if layer == 0 else dual[0, layer - 1]
        values[layer] = field[layer] + 0.25 * (
            (dual[0, layer] - prev) + flux(dual[1, layer], dual[2, layer], before[layer : layer + 1, :])
        )
    side = jnp.where(row_ids() == 0, spread_row(before[8:9, :]), 0.0)
    values[LAYERS] = below[16:32, :] - 0.25 * (dual[0, LAYERS - 1] + side)


def ramps(depth, base):
    away = depth - base
    return away * (0.5 * STEP * (BINS - 1) / BAND) + 0.5 * STEP * (BINS - 1), away * (STEP / BAND) + 2.0 * STEP


def votes(views, caps, layer):
    sums, places, weights = None, None, None
    for (place, weight), cap in zip(views, caps):
        q = jnp.clip(place - layer * (0.5 * STEP * (BINS - 1) / BAND), 0.0, STEP * (BINS - 1))
        w = jnp.minimum(jnp.maximum(weight - layer * (STEP / BAND), 0.0), cap)
        e = q + w
        parts = [jnp.maximum(q, jnp.minimum(e, STEP * index)) for index in range(1, BINS)]
        sums = parts if sums is None else [total + part for total, part in zip(sums, parts)]
        places = q if places is None else places + q
        weights = w if weights is None else weights + w
    return sums, places, weights


def proximal(values, sums, places, weights):
    high = values + 0.5 * weights
    best = jnp.maximum(jnp.minimum(high, -1.0), values - 0.5 * weights)
    high = high + places
    for index in range(1, BINS):
        best = jnp.maximum(best, jnp.minimum(high - sums[index - 1], -1.0 + 2.0 * index / (BINS - 1)))
    return best


def block_of(index):
    half, column = index // 8, index % 8
    return half, column, pl.ds(pl.multiple_of(half * 8, 8), 8), pl.ds(pl.multiple_of(column * 128, 128), 128)


def slab_base():
    return (lax.axis_index("slab") * LAYERS).astype(jnp.float32)


def first_update(visible, field, values, below, batches, updated, extra, side):
    base = slab_base()
    caps = [STEP * visible[view].astype(jnp.float32) for view in range(VIEWS)]

    def body(index, carry):
        half, column, rows, lanes = block_of(index)
        views = [ramps(batches[2 * view + half, column], base) for view in range(VIEWS)]
        for layer in range(LAYERS + 1):
            new = proximal(values[layer, rows, lanes], *votes(views, caps, float(layer)))
            if layer < LAYERS:
                updated[layer, rows, lanes] = new
                extra[layer, rows, lanes] = 2.0 * new - field[layer, rows, lanes]
            else:
                extra[layer, rows, lanes] = 2.0 * new - below[rows, lanes]
        return carry

    lax.fori_loop(0, 16, body, 0)
    for layer in range(LAYERS):
        side[layer : layer + 1, :] = extra[layer, 0:1, :]


def second_duals(extra, dual, ahead, new_dual, top, side):
    slab_end = lax.axis_index("slab") == Z_LAST
    for layer in range(LAYERS):
        last = layer == LAYERS - 1
        dual_z, dual_x, dual_y = dual_layer(
            extra[layer],
            extra[layer + 1],
            ahead[layer : layer + 1, :],
            dual[0, layer],
            dual[1, layer],
            dual[2, layer],
            slab_end if last else False,
        )
        new_dual[0, layer] = dual_z
        new_dual[1, layer] = dual_x
        new_dual[2, layer] = dual_y
        side[layer : layer + 1, :] = dual_x[15:16, :]
        if last:
            top[...] = dual_z


def all_votes(visible, batches, after, tally):
    base = slab_base()
    caps = [STEP * visible[view].astype(jnp.float32) for view in range(ITERS * VIEWS)]

    def body(index, carry):
        half, column, rows, lanes = block_of(index)
        views = [ramps(batches[2 * view + half, column], base) for view in range(ITERS * VIEWS)]
        for layer in range(LAYERS):
            sums, places, weights = votes(views, caps, float(layer))
            for slot, total in enumerate(sums + [places, weights]):
                tally[slot, layer, rows, lanes] = total
        return carry

    lax.fori_loop(0, 16, body, 0)


def last_update(current, dual, above, before, tally, updated):
    for layer in range(LAYERS):
        prev = above[...] if layer == 0 else dual[0, layer - 1]
        values = current[layer] + 0.25 * (
            (dual[0, layer] - prev) + flux(dual[1, layer], dual[2, layer], before[layer : layer + 1, :])
        )
        sums = [tally[slot, layer] for slot in range(BINS - 1)]
        updated[layer] = proximal(values, sums, tally[BINS - 1, layer], tally[BINS, layer])


def passed_along(value, axis, steps):
    count = lax.axis_size(axis)
    first, last = (max(0, -steps), min(count, count - steps))
    return lax.ppermute(value, axis, [(source, source + steps) for source in range(first, last)])


GROUPS = [[2 * place + half for place in range(16)] for half in range(2)]


def exchange(pieces):
    return lax.all_to_all(pieces, "slab", 0, 0, axis_index_groups=GROUPS)


def per_device(field, dual, depth, owner, visible):
    slab = lax.axis_index("slab")
    seen = visible.reshape(ITERS * VIEWS)
    block = (LAYERS, ROWS, LANES)

    pieces = depth.reshape(16, 8, 8, 128).transpose(0, 2, 1, 3)
    spread = exchange(pieces)

    ahead = passed_along(field[:, 0], "tile", -1)
    (message,) = call(first_layer, [(40, LANES)], 1 << 19, [VMEM] * 3)(field[0:2], dual[:, 0:1], ahead)

    root = owner[slab // 16]
    kept = lax.dynamic_index_in_dim(spread, root // 2, 0, keepdims=False)
    kept, _ = lax.optimization_barrier((kept, message))
    across = lax.ppermute(kept, "slab", [(index, index ^ 1) for index in range(32)])
    below = passed_along(message, "slab", -1)
    dual, top, side = call(all_duals, [(3,) + block, (ROWS, LANES), (ROWS, LANES)], 1 << 22, [VMEM] * 4)(
        field, dual, ahead, below
    )
    across, top, side = lax.optimization_barrier((across, top, side))
    kept = jnp.where(root % 2 == slab % 2, kept, across)
    batches = exchange(jnp.broadcast_to(kept[None], pieces.shape))
    before = passed_along(side, "tile", 1)
    above = passed_along(top, "slab", 1)
    (values,) = call(all_steps, [(LAYERS + 1, ROWS, LANES)], 1 << 21, [VMEM] * 5)(field, dual, above, before, below)

    current, extra, side = call(
        first_update, [block, (LAYERS + 1, ROWS, LANES), (LAYERS, LANES)], 1 << 24, [SMEM] + [VMEM] * 4
    )(seen, field, values, below, batches)
    ahead = passed_along(side, "tile", -1)
    dual, top, side = call(second_duals, [(3,) + block, (ROWS, LANES), (LAYERS, LANES)], 1 << 22, [VMEM] * 3)(
        extra, dual, ahead
    )
    before = passed_along(side, "tile", 1)
    above = passed_along(top, "slab", 1)
    (tally,) = call(all_votes, [(BINS + 1,) + block], 1 << 25, [SMEM, VMEM, ANY])(seen, batches, dual)
    (current,) = call(last_update, [block], 1 << 22, [VMEM] * 5)(current, dual, above, before, tally)
    return (current, dual)


def solution(mesh):
    placed = (
        P("slab", "tile", None),
        P(None, "slab", "tile", None),
        P("slab", None, None, "tile", None),
        P(),
        P(None, None, "tile"),
    )
    return jax.shard_map(
        per_device,
        mesh=mesh,
        in_specs=placed,
        out_specs=(P("slab", "tile", None), P(None, "slab", "tile", None)),
        check_vma=False,
    )
```

```python
import jax
import jax.numpy as jnp
from jax import lax
from jax.experimental import pallas as pl
from jax.experimental.pallas import tpu as pltpu
from jax.sharding import PartitionSpec as P

VIEWS = 4
BINS = 8
BAND = 6
ITERS = 2

LAYERS = 8
ROWS = 16
LANES = 1024
STEP = 0.1
Z_LAST = 31
X_LAST = 15


def call(kernel, out_shapes, cost_us, in_specs, **more):
    return pl.pallas_call(
        kernel,
        out_shape=tuple(jax.ShapeDtypeStruct(shape, jnp.float32) for shape in out_shapes),
        in_specs=in_specs,
        compiler_params=pltpu.CompilerParams(vmem_limit_bytes=16 << 20),
        cost_estimate=pl.CostEstimate(flops=0, transcendentals=0, bytes_accessed=int(cost_us * 3.0e6)),
        name=kernel.__name__,
        **more,
    )


VMEM = pl.BlockSpec(memory_space=pltpu.VMEM)
SMEM = pl.BlockSpec(memory_space=pltpu.SMEM)
ANY = pl.BlockSpec(memory_space=pl.ANY)


def row_ids():
    return lax.broadcasted_iota(jnp.int32, (ROWS, LANES), 0)


def lane_ids():
    return lax.broadcasted_iota(jnp.int32, (ROWS, LANES), 1)


def spread_row(row):
    return jnp.broadcast_to(row, (ROWS, LANES))


def dual_layer(here, ahead_z, ahead_row, dual_z, dual_x, dual_y, z_end):
    row, lane = row_ids(), lane_ids()
    x_end = (row == ROWS - 1) & (lax.axis_index("tile") == X_LAST)
    y_end = lane == LANES - 1
    ahead_x = jnp.where(row == ROWS - 1, spread_row(ahead_row), pltpu.roll(here, ROWS - 1, 0))
    ahead_y = pltpu.roll(here, LANES - 1, 1)
    moved_z = dual_z + 0.25 * jnp.where(z_end, 0.0, ahead_z - here)
    moved_x = dual_x + 0.25 * jnp.where(x_end, 0.0, ahead_x - here)
    moved_y = dual_y + 0.25 * jnp.where(y_end, 0.0, ahead_y - here)
    norm = moved_z * moved_z + moved_x * moved_x + moved_y * moved_y
    scale = 1.0 / jnp.sqrt(jnp.maximum(norm, 1.0))
    return (
        jnp.where(z_end, 0.0, moved_z * scale),
        jnp.where(x_end, 0.0, moved_x * scale),
        jnp.where(y_end, 0.0, moved_y * scale),
    )


def flux(dual_x, dual_y, before_row):
    before = jnp.where(row_ids() == 0, spread_row(before_row), pltpu.roll(dual_x, 1, 0))
    return (dual_x - before) + (dual_y - pltpu.roll(dual_y, 1, 1))


def first_layer(field, dual, ahead, message):
    here = field[0]
    dual_z, dual_x, dual_y = dual_layer(here, field[1], ahead[0:1, :], dual[0, 0], dual[1, 0], dual[2, 0], False)
    message[0:16, :] = here
    message[16:32, :] = here + 0.25 * (dual_z + flux(dual_x, dual_y, jnp.zeros((1, LANES), jnp.float32)))
    message[32:40, :] = dual_x[8:16, :]


def all_duals(field, dual, ahead, below, new_dual, top, side):
    slab_end = lax.axis_index("slab") == Z_LAST
    for layer in range(LAYERS):
        last = layer == LAYERS - 1
        dual_z, dual_x, dual_y = dual_layer(
            field[layer],
            below[0:16, :] if last else field[layer + 1],
            ahead[layer : layer + 1, :],
            dual[0, layer],
            dual[1, layer],
            dual[2, layer],
            slab_end if last else False,
        )
        new_dual[0, layer] = dual_z
        new_dual[1, layer] = dual_x
        new_dual[2, layer] = dual_y
        side[layer : layer + 1, :] = dual_x[15:16, :]
        if last:
            top[...] = dual_z
    side[8:16, :] = jnp.zeros((8, LANES), jnp.float32)
    side[8:9, :] = below[39:40, :]


def ramps(depth, base):
    away = depth - base
    return away * (0.5 * STEP * (BINS - 1) / BAND) + 0.5 * STEP * (BINS - 1), away * (STEP / BAND) + 2.0 * STEP


def votes(views, caps, layer):
    sums, places, weights = None, None, None
    for (place, weight), cap in zip(views, caps):
        q = jnp.clip(place - layer * (0.5 * STEP * (BINS - 1) / BAND), 0.0, STEP * (BINS - 1))
        w = jnp.minimum(jnp.maximum(weight - layer * (STEP / BAND), 0.0), cap)
        e = q + w
        parts = [jnp.maximum(q, jnp.minimum(e, STEP * index)) for index in range(1, BINS)]
        sums = parts if sums is None else [total + part for total, part in zip(sums, parts)]
        places = q if places is None else places + q
        weights = w if weights is None else weights + w
    return sums, places, weights


def proximal(values, sums, places, weights):
    high = values + 0.5 * weights
    best = jnp.maximum(jnp.minimum(high, -1.0), values - 0.5 * weights)
    high = high + places
    for index in range(1, BINS):
        best = jnp.maximum(best, jnp.minimum(high - sums[index - 1], -1.0 + 2.0 * index / (BINS - 1)))
    return best


def block_of(index):
    half, column = index // 8, index % 8
    return half, column, pl.ds(pl.multiple_of(half * 8, 8), 8), pl.ds(pl.multiple_of(column * 128, 128), 128)


def slab_base():
    return (lax.axis_index("slab") * LAYERS).astype(jnp.float32)


def first_votes(visible, batches, tally):
    base = slab_base()
    caps = [STEP * visible[view].astype(jnp.float32) for view in range(VIEWS)]

    def body(index, carry):
        half, column, rows, lanes = block_of(index)
        views = [ramps(batches[2 * view + half, column], base) for view in range(VIEWS)]
        for layer in range(LAYERS + 1):
            sums, places, weights = votes(views, caps, float(layer))
            for slot, total in enumerate(sums + [places, weights]):
                tally[slot, layer, rows, lanes] = total
        return carry

    lax.fori_loop(0, 16, body, 0)


def second_votes(visible, batches, tally, after, new_tally):
    base = slab_base()
    caps = [STEP * visible[VIEWS + view].astype(jnp.float32) for view in range(VIEWS)]

    def body(index, carry):
        half, column, rows, lanes = block_of(index)
        views = [ramps(batches[2 * (VIEWS + view) + half, column], base) for view in range(VIEWS)]
        for layer in range(LAYERS):
            sums, places, weights = votes(views, caps, float(layer))
            for slot, total in enumerate(sums + [places, weights]):
                new_tally[slot, layer, rows, lanes] = tally[slot, layer, rows, lanes] + total
        return carry

    lax.fori_loop(0, 16, body, 0)


def counted(values, tally, layer):
    sums = [tally[slot, layer] for slot in range(BINS - 1)]
    return proximal(values, sums, tally[BINS - 1, layer], tally[BINS, layer])


def stepped(field, dual, above, before, layer):
    prev = above[...] if layer == 0 else dual[0, layer - 1]
    return field[layer] + 0.25 * (
        (dual[0, layer] - prev) + flux(dual[1, layer], dual[2, layer], before[layer : layer + 1, :])
    )


def first_update(field, dual, above, before, below, tally, updated, extra, side):
    for layer in range(LAYERS):
        new = counted(stepped(field, dual, above, before, layer), tally, layer)
        updated[layer] = new
        new = 2.0 * new - field[layer]
        extra[layer] = new
        side[layer : layer + 1, :] = new[0:1, :]
    past = jnp.where(row_ids() == 0, spread_row(before[8:9, :]), 0.0)
    values = below[16:32, :] - 0.25 * (dual[0, LAYERS - 1] + past)
    extra[LAYERS] = 2.0 * counted(values, tally, LAYERS) - below[0:16, :]


def top_dual(extra, dual, ahead, top):
    layer = LAYERS - 1
    slab_end = lax.axis_index("slab") == Z_LAST
    top[...] = dual_layer(
        extra[0], extra[1], ahead[layer : layer + 1, :], dual[0, 0], dual[1, 0], dual[2, 0], slab_end
    )[0]


def second_duals(extra, dual, ahead, after, new_dual, side):
    slab_end = lax.axis_index("slab") == Z_LAST
    for layer in range(LAYERS):
        last = layer == LAYERS - 1
        dual_z, dual_x, dual_y = dual_layer(
            extra[layer],
            extra[layer + 1],
            ahead[layer : layer + 1, :],
            dual[0, layer],
            dual[1, layer],
            dual[2, layer],
            slab_end if last else False,
        )
        new_dual[0, layer] = dual_z
        new_dual[1, layer] = dual_x
        new_dual[2, layer] = dual_y
        side[layer : layer + 1, :] = dual_x[15:16, :]


def last_layers(current, dual, before, tally, updated):
    for layer in range(1, LAYERS):
        updated[layer] = counted(stepped(current, dual, None, before, layer), tally, layer)


def last_layer(current, dual, above, before, tally, updated_in, updated):
    updated[0] = counted(stepped(current, dual, above, before, 0), tally, 0)


def passed_along(value, axis, steps):
    count = lax.axis_size(axis)
    first, last = (max(0, -steps), min(count, count - steps))
    return lax.ppermute(value, axis, [(source, source + steps) for source in range(first, last)])


GROUPS = [[2 * place + half for place in range(16)] for half in range(2)]


def exchange(pieces):
    return lax.all_to_all(pieces, "slab", 0, 0, axis_index_groups=GROUPS)


def per_device(field, dual, depth, owner, visible):
    slab = lax.axis_index("slab")
    seen = visible.reshape(ITERS * VIEWS)
    block = (LAYERS, ROWS, LANES)

    first_one = pl.BlockSpec((1, ROWS, LANES), lambda step: (0, 0, 0))
    first_one_dual = pl.BlockSpec((3, 1, ROWS, LANES), lambda step: (0, 0, 0, 0))
    tally_one = pl.BlockSpec((BINS + 1, 1, ROWS, LANES), lambda step: (0, 0, 0, 0))
    first = pl.BlockSpec((2, ROWS, LANES), lambda step: (0, 0, 0))

    pieces = depth.reshape(16, 8, 8, 128).transpose(0, 2, 1, 3)
    spread = exchange(pieces)

    ahead = passed_along(field[:, 0], "tile", -1)
    (message,) = call(first_layer, [(40, LANES)], 1, [first, first_one_dual, VMEM], grid=(1,))(field, dual, ahead)

    root = owner[slab // 16]
    kept = lax.dynamic_index_in_dim(spread, root // 2, 0, keepdims=False)
    kept, _ = lax.optimization_barrier((kept, message))
    across = lax.ppermute(kept, "slab", [(index, index ^ 1) for index in range(32)])
    below = passed_along(message, "slab", -1)
    dual, top, side = call(all_duals, [(3,) + block, (ROWS, LANES), (ROWS, LANES)], 1, [VMEM] * 4)(
        field, dual, ahead, below
    )
    across, top, side = lax.optimization_barrier((across, top, side))
    kept = jnp.where(root % 2 == slab % 2, kept, across)
    batches = exchange(jnp.broadcast_to(kept[None], pieces.shape))
    before = passed_along(side, "tile", 1)
    above = passed_along(top, "slab", 1)

    (tally,) = call(first_votes, [(BINS + 1, LAYERS + 1, ROWS, LANES)], 4, [SMEM, VMEM])(seen, batches)
    above, before, tally = lax.optimization_barrier((above, before, tally))
    current, extra, side = call(first_update, [block, (LAYERS + 1, ROWS, LANES), (LAYERS, LANES)], 1, [VMEM] * 6)(
        field, dual, above, before, below, tally
    )
    ahead = passed_along(side, "tile", -1)
    (top,) = call(top_dual, [(ROWS, LANES)], 1, [VMEM] * 3)(extra[7:9], dual[:, 7:8], ahead)
    above = passed_along(top, "slab", 1)
    dual, side = call(second_duals, [(3,) + block, (LAYERS, LANES)], 1, [VMEM] * 3 + [ANY])(extra, dual, ahead, top)
    before = passed_along(side, "tile", 1)
    (tally,) = call(second_votes, [(BINS + 1,) + block], 3, [SMEM, VMEM, VMEM, ANY])(seen, batches, tally, dual)
    (rest,) = call(last_layers, [block], 1, [VMEM] * 4)(current, dual, before, tally)
    above, rest = lax.optimization_barrier((above, rest))
    (current,) = call(
        last_layer, [block], 1, [first_one, first_one_dual, VMEM, VMEM, tally_one, ANY], grid=(1,),
        out_specs=(first_one,), input_output_aliases={5: 0},
    )(current, dual, above, before, tally, rest)
    return (current, dual)


def solution(mesh):
    placed = (
        P("slab", "tile", None),
        P(None, "slab", "tile", None),
        P("slab", None, None, "tile", None),
        P(),
        P(None, None, "tile"),
    )
    return jax.shard_map(
        per_device,
        mesh=mesh,
        in_specs=placed,
        out_specs=(P("slab", "tile", None), P(None, "slab", "tile", None)),
        check_vma=False,
    )
```

```python
import jax
import jax.numpy as jnp
from jax import lax
from jax.experimental import pallas as pl
from jax.experimental.pallas import tpu as pltpu
from jax.sharding import PartitionSpec as P

VIEWS = 4
BINS = 8
BAND = 6
ITERS = 2

LAYERS = 8
ROWS = 16
LANES = 1024
STEP = 0.1
Z_LAST = 31
X_LAST = 15


def call(kernel, out_shapes, cost_us, in_specs, **more):
    return pl.pallas_call(
        kernel,
        out_shape=tuple(jax.ShapeDtypeStruct(shape, jnp.float32) for shape in out_shapes),
        in_specs=in_specs,
        compiler_params=pltpu.CompilerParams(vmem_limit_bytes=16 << 20),
        cost_estimate=pl.CostEstimate(flops=0, transcendentals=0, bytes_accessed=int(cost_us * 3.0e6)),
        name=kernel.__name__,
        **more,
    )


VMEM = pl.BlockSpec(memory_space=pltpu.VMEM)
SMEM = pl.BlockSpec(memory_space=pltpu.SMEM)
HBM = pl.BlockSpec(memory_space=pltpu.HBM)
ANY = pl.BlockSpec(memory_space=pl.ANY)


def row_ids():
    return lax.broadcasted_iota(jnp.int32, (ROWS, LANES), 0)


def lane_ids():
    return lax.broadcasted_iota(jnp.int32, (ROWS, LANES), 1)


def spread_row(row):
    return jnp.broadcast_to(row, (ROWS, LANES))


def ends():
    row, lane = row_ids(), lane_ids()
    return row, (row == ROWS - 1) & (lax.axis_index("tile") == X_LAST), lane == LANES - 1


def moved_sides(here, ahead_row, dual_x, dual_y):
    row, x_end, y_end = ends()
    ahead_x = jnp.where(row == ROWS - 1, spread_row(ahead_row), pltpu.roll(here, ROWS - 1, 0))
    ahead_y = pltpu.roll(here, LANES - 1, 1)
    moved_x = dual_x + 0.25 * jnp.where(x_end, 0.0, ahead_x - here)
    return moved_x, dual_y + 0.25 * jnp.where(y_end, 0.0, ahead_y - here)


def dual_layer(here, ahead_z, ahead_row, dual_z, dual_x, dual_y, z_end):
    _, x_end, y_end = ends()
    moved_z = dual_z + 0.25 * jnp.where(z_end, 0.0, ahead_z - here)
    moved_x, moved_y = moved_sides(here, ahead_row, dual_x, dual_y)
    norm = moved_z * moved_z + moved_x * moved_x + moved_y * moved_y
    scale = 1.0 / jnp.sqrt(jnp.maximum(norm, 1.0))
    return (
        jnp.where(z_end, 0.0, moved_z * scale),
        jnp.where(x_end, 0.0, moved_x * scale),
        jnp.where(y_end, 0.0, moved_y * scale),
    )


def flux(dual_x, dual_y, before_row):
    before = jnp.where(row_ids() == 0, spread_row(before_row), pltpu.roll(dual_x, 1, 0))
    return (dual_x - before) + (dual_y - pltpu.roll(dual_y, 1, 1))


def pick(owner, spread, kept):
    kept[...] = spread[lax.shift_right_logical(owner[lax.shift_right_logical(lax.axis_index("slab"), 4)], 1)]


def copies_of(owner, kept, across, copies):
    slab = lax.axis_index("slab")
    here = (owner[lax.shift_right_logical(slab, 4)] & 1) == (slab & 1)
    piece = jnp.where(here, kept[...], across[...])
    for place in range(16):
        copies[place] = piece


def end_layers(field, dual, ahead, down, up, layers, duals, sems):
    copies = [
        pltpu.make_async_copy(field.at[0:2], layers.at[0:2], sems.at[0]),
        pltpu.make_async_copy(dual.at[:, 0], duals.at[0], sems.at[1]),
        pltpu.make_async_copy(field.at[LAYERS - 1], layers.at[2], sems.at[2]),
        pltpu.make_async_copy(dual.at[:, LAYERS - 1], duals.at[1], sems.at[3]),
    ]
    for copy in copies:
        copy.start()
    for copy in copies:
        copy.wait()
    here = layers[0]
    dual_z, dual_x, dual_y = dual_layer(here, layers[1], ahead[0:1, :], duals[0, 0], duals[0, 1], duals[0, 2], False)
    down[0:16, :] = here
    down[16:32, :] = here + 0.25 * (dual_z + flux(dual_x, dual_y, jnp.zeros((1, LANES), jnp.float32)))
    down[32:40, :] = dual_x[8:16, :]
    moved_x, moved_y = moved_sides(layers[2], ahead[7:8, :], duals[1, 1], duals[1, 2])
    up[0:16, :] = duals[1, 0] - 0.25 * layers[2]
    up[16:32, :] = moved_x * moved_x + moved_y * moved_y


def top_of(up, here):
    moved = up[0:16, :] + 0.25 * here
    scale = 1.0 / jnp.sqrt(jnp.maximum(moved * moved + up[16:32, :], 1.0))
    return jnp.where(lax.axis_index("slab") == 0, 0.0, moved * scale)


def all_duals(field, dual, ahead, below, up, new_dual, top, side):
    slab_end = lax.axis_index("slab") == Z_LAST
    for layer in range(LAYERS):
        last = layer == LAYERS - 1
        dual_z, dual_x, dual_y = dual_layer(
            field[layer],
            below[0:16, :] if last else field[layer + 1],
            ahead[layer : layer + 1, :],
            dual[0, layer],
            dual[1, layer],
            dual[2, layer],
            slab_end if last else False,
        )
        new_dual[0, layer] = dual_z
        new_dual[1, layer] = dual_x
        new_dual[2, layer] = dual_y
        side[layer : layer + 1, :] = dual_x[15:16, :]
    top[...] = top_of(up, field[0])
    side[8:16, :] = jnp.zeros((8, LANES), jnp.float32)
    side[8:9, :] = below[39:40, :]


def ramps(depth, base):
    away = depth - base
    return away * (0.5 * STEP * (BINS - 1) / BAND) + 0.5 * STEP * (BINS - 1), away * (STEP / BAND) + 2.0 * STEP


def votes(views, caps, layer):
    sums, places, weights = None, None, None
    for (place, weight), cap in zip(views, caps):
        q = jnp.clip(place - layer * (0.5 * STEP * (BINS - 1) / BAND), 0.0, STEP * (BINS - 1))
        w = jnp.minimum(jnp.maximum(weight - layer * (STEP / BAND), 0.0), cap)
        e = q + w
        parts = [jnp.maximum(q, jnp.minimum(e, STEP * index)) for index in range(1, BINS)]
        sums = parts if sums is None else [total + part for total, part in zip(sums, parts)]
        places = q if places is None else places + q
        weights = w if weights is None else weights + w
    return sums, places, weights


def proximal(values, sums, places, weights):
    high = values + 0.5 * weights
    best = jnp.maximum(jnp.minimum(high, -1.0), values - 0.5 * weights)
    high = high + places
    for index in range(1, BINS):
        best = jnp.maximum(best, jnp.minimum(high - sums[index - 1], -1.0 + 2.0 * index / (BINS - 1)))
    return best


def block_of(index):
    half, column = index // 8, index % 8
    return half, column, pl.ds(pl.multiple_of(half * 8, 8), 8), pl.ds(pl.multiple_of(column * 128, 128), 128)


def slab_base():
    return (lax.axis_index("slab") * LAYERS).astype(jnp.float32)


def first_votes(visible, batches, tally):
    base = slab_base()
    caps = [STEP * visible[0, view, 0].astype(jnp.float32) for view in range(VIEWS)]

    def body(index, carry):
        half, column, rows, lanes = block_of(index)
        views = [ramps(batches[2 * view + half, column], base) for view in range(VIEWS)]
        for layer in range(LAYERS + 1):
            sums, places, weights = votes(views, caps, float(layer))
            for slot, total in enumerate(sums + [places, weights]):
                tally[slot, layer, rows, lanes] = total
        return carry

    lax.fori_loop(0, 16, body, 0)


def second_votes(visible, batches, tally, after, new_tally):
    base = slab_base()
    caps = [STEP * visible[1, view, 0].astype(jnp.float32) for view in range(VIEWS)]

    def body(index, carry):
        half, column, rows, lanes = block_of(index)
        views = [ramps(batches[2 * (VIEWS + view) + half, column], base) for view in range(VIEWS)]
        for layer in range(LAYERS):
            sums, places, weights = votes(views, caps, float(layer))
            for slot, total in enumerate(sums + [places, weights]):
                new_tally[slot, layer, rows, lanes] = tally[slot, layer, rows, lanes] + total
        return carry

    lax.fori_loop(0, 16, body, 0)


def counted(values, tally, layer):
    sums = [tally[slot, layer] for slot in range(BINS - 1)]
    return proximal(values, sums, tally[BINS - 1, layer], tally[BINS, layer])


def stepped(field, dual, above, before, layer):
    prev = above[...] if layer == 0 else dual[0, layer - 1]
    return field[layer] + 0.25 * (
        (dual[0, layer] - prev) + flux(dual[1, layer], dual[2, layer], before[layer : layer + 1, :])
    )


def first_update(field, dual, above, before, below, tally, updated, extra, side):
    for layer in range(LAYERS):
        new = counted(stepped(field, dual, above, before, layer), tally, layer)
        updated[layer] = new
        new = 2.0 * new - field[layer]
        extra[layer] = new
        side[layer : layer + 1, :] = new[0:1, :]
    past = jnp.where(row_ids() == 0, spread_row(before[8:9, :]), 0.0)
    values = below[16:32, :] - 0.25 * (dual[0, LAYERS - 1] + past)
    extra[LAYERS] = 2.0 * counted(values, tally, LAYERS) - below[0:16, :]


def top_dual(extra, dual, ahead, top):
    layer = LAYERS - 1
    slab_end = lax.axis_index("slab") == Z_LAST
    top[...] = dual_layer(
        extra[0], extra[1], ahead[layer : layer + 1, :], dual[0, 0], dual[1, 0], dual[2, 0], slab_end
    )[0]


def second_duals(extra, dual, ahead, after, new_dual, side):
    slab_end = lax.axis_index("slab") == Z_LAST
    for layer in range(LAYERS):
        last = layer == LAYERS - 1
        dual_z, dual_x, dual_y = dual_layer(
            extra[layer],
            extra[layer + 1],
            ahead[layer : layer + 1, :],
            dual[0, layer],
            dual[1, layer],
            dual[2, layer],
            slab_end if last else False,
        )
        new_dual[0, layer] = dual_z
        new_dual[1, layer] = dual_x
        new_dual[2, layer] = dual_y
        side[layer : layer + 1, :] = dual_x[15:16, :]


def last_layers(current, dual, before, tally, updated):
    for layer in range(1, LAYERS):
        updated[layer] = counted(stepped(current, dual, None, before, layer), tally, layer)


def last_layer(current, dual, above, before, tally, updated_in, updated):
    updated[0] = counted(stepped(current, dual, above, before, 0), tally, 0)


def passed_along(value, axis, steps):
    count = lax.axis_size(axis)
    first, last = (max(0, -steps), min(count, count - steps))
    return lax.ppermute(value, axis, [(source, source + steps) for source in range(first, last)])


GROUPS = [[2 * place + half for place in range(16)] for half in range(2)]


def exchange(pieces):
    return lax.all_to_all(pieces, "slab", 0, 0, axis_index_groups=GROUPS)


def per_device(field, dual, depth, owner, visible):
    block = (LAYERS, ROWS, LANES)

    first_one = pl.BlockSpec((1, ROWS, LANES), lambda step: (0, 0, 0))
    first_one_dual = pl.BlockSpec((3, 1, ROWS, LANES), lambda step: (0, 0, 0, 0))
    tally_one = pl.BlockSpec((BINS + 1, 1, ROWS, LANES), lambda step: (0, 0, 0, 0))

    pieces = depth.reshape(16, 8, 8, 128).transpose(0, 2, 1, 3)
    spread = exchange(pieces)

    ahead = passed_along(field[:, 0], "tile", -1)
    down, up = call(
        end_layers, [(40, LANES), (32, LANES)], 1, [HBM, HBM, VMEM],
        scratch_shapes=[
            pltpu.VMEM((3, ROWS, LANES), jnp.float32),
            pltpu.VMEM((2, 3, ROWS, LANES), jnp.float32),
            pltpu.SemaphoreType.DMA((4,)),
        ],
    )(pltpu.with_memory_space_constraint(field, pltpu.HBM), pltpu.with_memory_space_constraint(dual, pltpu.HBM), ahead)
    (kept,) = call(pick, [(8, 8, 128)], 1, [SMEM, VMEM])(owner, spread)
    kept, _ = lax.optimization_barrier((kept, down))
    across = lax.ppermute(kept, "slab", [(index, index ^ 1) for index in range(32)])
    below = passed_along(down, "slab", -1)
    above = passed_along(up, "slab", 1)
    across, below, above = lax.optimization_barrier((across, below, above))
    (copies,) = call(copies_of, [pieces.shape], 1, [SMEM, VMEM, VMEM])(owner, kept, across)
    batches = exchange(copies)
    below, _ = lax.optimization_barrier((below, copies))
    dual, above, side = call(all_duals, [(3,) + block, (ROWS, LANES), (ROWS, LANES)], 1, [VMEM] * 5)(
        field, dual, ahead, below, above
    )
    before = passed_along(side, "tile", 1)

    (tally,) = call(first_votes, [(BINS + 1, LAYERS + 1, ROWS, LANES)], 4, [SMEM, VMEM])(visible, batches)
    before, tally = lax.optimization_barrier((before, tally))
    current, extra, side = call(first_update, [block, (LAYERS + 1, ROWS, LANES), (LAYERS, LANES)], 1, [VMEM] * 6)(
        field, dual, above, before, below, tally
    )
    ahead = passed_along(side, "tile", -1)
    (top,) = call(top_dual, [(ROWS, LANES)], 1, [VMEM] * 3)(extra[7:9], dual[:, 7:8], ahead)
    above = passed_along(top, "slab", 1)
    dual, side = call(second_duals, [(3,) + block, (LAYERS, LANES)], 1, [VMEM] * 3 + [ANY])(extra, dual, ahead, top)
    before = passed_along(side, "tile", 1)
    (tally,) = call(second_votes, [(BINS + 1,) + block], 3, [SMEM, VMEM, VMEM, ANY])(visible, batches, tally, side)
    (rest,) = call(last_layers, [block], 1, [VMEM] * 4)(current, dual, before, tally)
    above, rest = lax.optimization_barrier((above, rest))
    (current,) = call(
        last_layer, [block], 1, [first_one, first_one_dual, VMEM, VMEM, tally_one, ANY], grid=(1,),
        out_specs=(first_one,), input_output_aliases={5: 0},
    )(current, dual, above, before, tally, rest)
    return (current, dual)


def solution(mesh):
    placed = (
        P("slab", "tile", None),
        P(None, "slab", "tile", None),
        P("slab", None, None, "tile", None),
        P(),
        P(None, None, "tile"),
    )
    return jax.shard_map(
        per_device,
        mesh=mesh,
        in_specs=placed,
        out_specs=(P("slab", "tile", None), P(None, "slab", "tile", None)),
        check_vma=False,
    )
```

```python
import jax
import jax.numpy as jnp
from jax import lax
from jax.experimental import pallas as pl
from jax.experimental.pallas import tpu as pltpu
from jax.sharding import PartitionSpec as P

VIEWS = 4
BINS = 8
BAND = 6
ITERS = 2

LAYERS = 8
ROWS = 16
LANES = 1024
STEP = 0.1
Z_LAST = 31
X_LAST = 15


def call(kernel, out_shapes, cost_us, in_specs, **more):
    return pl.pallas_call(
        kernel,
        out_shape=tuple(jax.ShapeDtypeStruct(shape, jnp.float32) for shape in out_shapes),
        in_specs=in_specs,
        compiler_params=pltpu.CompilerParams(vmem_limit_bytes=16 << 20),
        cost_estimate=pl.CostEstimate(flops=int(cost_us * 1.0e9), transcendentals=0, bytes_accessed=int(cost_us * 3.0e6)),
        name=kernel.__name__,
        **more,
    )


VMEM = pl.BlockSpec(memory_space=pltpu.VMEM)
SMEM = pl.BlockSpec(memory_space=pltpu.SMEM)
HBM = pl.BlockSpec(memory_space=pltpu.HBM)
ANY = pl.BlockSpec(memory_space=pl.ANY)


def row_ids():
    return lax.broadcasted_iota(jnp.int32, (ROWS, LANES), 0)


def lane_ids():
    return lax.broadcasted_iota(jnp.int32, (ROWS, LANES), 1)


def spread_row(row):
    return jnp.broadcast_to(row, (ROWS, LANES))


def ends():
    row, lane = row_ids(), lane_ids()
    return row, (row == ROWS - 1) & (lax.axis_index("tile") == X_LAST), lane == LANES - 1


def moved_sides(here, ahead_row, dual_x, dual_y):
    row, x_end, y_end = ends()
    ahead_x = jnp.where(row == ROWS - 1, spread_row(ahead_row), pltpu.roll(here, ROWS - 1, 0))
    ahead_y = pltpu.roll(here, LANES - 1, 1)
    moved_x = dual_x + 0.25 * jnp.where(x_end, 0.0, ahead_x - here)
    return moved_x, dual_y + 0.25 * jnp.where(y_end, 0.0, ahead_y - here)


def dual_layer(here, ahead_z, ahead_row, dual_z, dual_x, dual_y, z_end):
    _, x_end, y_end = ends()
    moved_z = dual_z + 0.25 * jnp.where(z_end, 0.0, ahead_z - here)
    moved_x, moved_y = moved_sides(here, ahead_row, dual_x, dual_y)
    norm = moved_z * moved_z + moved_x * moved_x + moved_y * moved_y
    scale = 1.0 / jnp.sqrt(jnp.maximum(norm, 1.0))
    return (
        jnp.where(z_end, 0.0, moved_z * scale),
        jnp.where(x_end, 0.0, moved_x * scale),
        jnp.where(y_end, 0.0, moved_y * scale),
    )


def flux(dual_x, dual_y, before_row):
    before = jnp.where(row_ids() == 0, spread_row(before_row), pltpu.roll(dual_x, 1, 0))
    return (dual_x - before) + (dual_y - pltpu.roll(dual_y, 1, 1))


def pick(owner, spread, kept):
    kept[...] = spread[lax.shift_right_logical(owner[lax.shift_right_logical(lax.axis_index("slab"), 4)], 1)]


def copies_of(owner, kept, across, copies):
    slab = lax.axis_index("slab")
    here = (owner[lax.shift_right_logical(slab, 4)] & 1) == (slab & 1)
    piece = jnp.where(here, kept[...], across[...])
    for place in range(16):
        copies[place] = piece


def first_layer(field, dual, ahead, down, layers, duals, sems):
    copies = [
        pltpu.make_async_copy(field.at[0:2], layers, sems.at[0]),
        pltpu.make_async_copy(dual.at[:, 0], duals, sems.at[1]),
    ]
    for copy in copies:
        copy.start()
    for copy in copies:
        copy.wait()
    here = layers[0]
    dual_z, dual_x, dual_y = dual_layer(here, layers[1], ahead[0:1, :], duals[0], duals[1], duals[2], False)
    down[0:16, :] = here
    down[16:32, :] = here + 0.25 * (dual_z + flux(dual_x, dual_y, jnp.zeros((1, LANES), jnp.float32)))
    down[32:40, :] = dual_x[8:16, :]


def all_duals(field, dual, ahead, below, new_dual, top, side):
    slab_end = lax.axis_index("slab") == Z_LAST
    for layer in range(LAYERS):
        last = layer == LAYERS - 1
        dual_z, dual_x, dual_y = dual_layer(
            field[layer],
            below[0:16, :] if last else field[layer + 1],
            ahead[layer : layer + 1, :],
            dual[0, layer],
            dual[1, layer],
            dual[2, layer],
            slab_end if last else False,
        )
        new_dual[0, layer] = dual_z
        new_dual[1, layer] = dual_x
        new_dual[2, layer] = dual_y
        side[layer : layer + 1, :] = dual_x[15:16, :]
    top[...] = new_dual[0, LAYERS - 1]
    side[8:16, :] = jnp.zeros((8, LANES), jnp.float32)
    side[8:9, :] = below[39:40, :]


def ramps(depth, base):
    away = depth - base
    return away * (0.5 * STEP * (BINS - 1) / BAND) + 0.5 * STEP * (BINS - 1), away * (STEP / BAND) + 2.0 * STEP


def votes(views, caps, layer):
    sums, places, weights = None, None, None
    for (place, weight), cap in zip(views, caps):
        q = jnp.clip(place - layer * (0.5 * STEP * (BINS - 1) / BAND), 0.0, STEP * (BINS - 1))
        w = jnp.minimum(jnp.maximum(weight - layer * (STEP / BAND), 0.0), cap)
        e = q + w
        parts = [jnp.maximum(q, jnp.minimum(e, STEP * index)) for index in range(1, BINS)]
        sums = parts if sums is None else [total + part for total, part in zip(sums, parts)]
        places = q if places is None else places + q
        weights = w if weights is None else weights + w
    return sums, places, weights


def proximal(values, sums, places, weights):
    high = values + 0.5 * weights
    best = jnp.maximum(jnp.minimum(high, -1.0), values - 0.5 * weights)
    high = high + places
    for index in range(1, BINS):
        best = jnp.maximum(best, jnp.minimum(high - sums[index - 1], -1.0 + 2.0 * index / (BINS - 1)))
    return best


def block_of(index):
    half, column = index // 8, index % 8
    return half, column, pl.ds(pl.multiple_of(half * 8, 8), 8), pl.ds(pl.multiple_of(column * 128, 128), 128)


def slab_base():
    return (lax.axis_index("slab") * LAYERS).astype(jnp.float32)


def first_votes(visible, batches, tally):
    base = slab_base()
    caps = [STEP * visible[0, view, 0].astype(jnp.float32) for view in range(VIEWS)]

    def body(index, carry):
        half, column, rows, lanes = block_of(index)
        views = [ramps(batches[2 * view + half, column], base) for view in range(VIEWS)]
        for layer in range(LAYERS + 1):
            sums, places, weights = votes(views, caps, float(layer))
            for slot, total in enumerate(sums + [places, weights]):
                tally[slot, layer, rows, lanes] = total
        return carry

    lax.fori_loop(0, 16, body, 0)


def second_votes(visible, batches, tally, after, new_tally):
    base = slab_base()
    caps = [STEP * visible[1, view, 0].astype(jnp.float32) for view in range(VIEWS)]

    def body(index, carry):
        half, column, rows, lanes = block_of(index)
        views = [ramps(batches[2 * (VIEWS + view) + half, column], base) for view in range(VIEWS)]
        for layer in range(LAYERS):
            sums, places, weights = votes(views, caps, float(layer))
            for slot, total in enumerate(sums + [places, weights]):
                new_tally[slot, layer, rows, lanes] = tally[slot, layer, rows, lanes] + total
        return carry

    lax.fori_loop(0, 16, body, 0)


def counted(values, tally, layer):
    sums = [tally[slot, layer] for slot in range(BINS - 1)]
    return proximal(values, sums, tally[BINS - 1, layer], tally[BINS, layer])


def stepped(field, dual, above, before, layer):
    prev = above[...] if layer == 0 else dual[0, layer - 1]
    return field[layer] + 0.25 * (
        (dual[0, layer] - prev) + flux(dual[1, layer], dual[2, layer], before[layer : layer + 1, :])
    )


def first_update(field, dual, above, before, below, tally, updated, extra, side):
    for layer in range(LAYERS):
        new = counted(stepped(field, dual, above, before, layer), tally, layer)
        updated[layer] = new
        new = 2.0 * new - field[layer]
        extra[layer] = new
        side[layer : layer + 1, :] = new[0:1, :]
    past = jnp.where(row_ids() == 0, spread_row(before[8:9, :]), 0.0)
    values = below[16:32, :] - 0.25 * (dual[0, LAYERS - 1] + past)
    extra[LAYERS] = 2.0 * counted(values, tally, LAYERS) - below[0:16, :]


def top_dual(extra, dual, ahead, top):
    layer = LAYERS - 1
    slab_end = lax.axis_index("slab") == Z_LAST
    top[...] = dual_layer(
        extra[0], extra[1], ahead[layer : layer + 1, :], dual[0, 0], dual[1, 0], dual[2, 0], slab_end
    )[0]


def second_duals(extra, dual, ahead, after, new_dual, side):
    slab_end = lax.axis_index("slab") == Z_LAST
    for layer in range(LAYERS):
        last = layer == LAYERS - 1
        dual_z, dual_x, dual_y = dual_layer(
            extra[layer],
            extra[layer + 1],
            ahead[layer : layer + 1, :],
            dual[0, layer],
            dual[1, layer],
            dual[2, layer],
            slab_end if last else False,
        )
        new_dual[0, layer] = dual_z
        new_dual[1, layer] = dual_x
        new_dual[2, layer] = dual_y
        side[layer : layer + 1, :] = dual_x[15:16, :]


def last_layers(current, dual, before, tally, updated):
    for layer in range(1, LAYERS):
        updated[layer] = counted(stepped(current, dual, None, before, layer), tally, layer)


def last_layer(current, dual, above, before, tally, updated_in, updated):
    updated[0] = counted(stepped(current, dual, above, before, 0), tally, 0)


def passed_along(value, axis, steps):
    count = lax.axis_size(axis)
    first, last = (max(0, -steps), min(count, count - steps))
    return lax.ppermute(value, axis, [(source, source + steps) for source in range(first, last)])


GROUPS = [[2 * place + half for place in range(16)] for half in range(2)]


def exchange(pieces):
    return lax.all_to_all(pieces, "slab", 0, 0, axis_index_groups=GROUPS)


def per_device(field, dual, depth, owner, visible):
    block = (LAYERS, ROWS, LANES)

    first_one = pl.BlockSpec((1, ROWS, LANES), lambda step: (0, 0, 0))
    first_one_dual = pl.BlockSpec((3, 1, ROWS, LANES), lambda step: (0, 0, 0, 0))
    tally_one = pl.BlockSpec((BINS + 1, 1, ROWS, LANES), lambda step: (0, 0, 0, 0))

    pieces = depth.reshape(16, 8, 8, 128).transpose(0, 2, 1, 3)
    spread = exchange(pieces)

    ahead = passed_along(field[:, 0], "tile", -1)
    (down,) = call(
        first_layer, [(40, LANES)], 1, [HBM, HBM, VMEM],
        scratch_shapes=[
            pltpu.VMEM((2, ROWS, LANES), jnp.float32),
            pltpu.VMEM((3, ROWS, LANES), jnp.float32),
            pltpu.SemaphoreType.DMA((2,)),
        ],
    )(pltpu.with_memory_space_constraint(field, pltpu.HBM), pltpu.with_memory_space_constraint(dual, pltpu.HBM), ahead)
    (kept,) = call(pick, [(8, 8, 128)], 1, [SMEM, VMEM])(owner, spread)
    kept, _ = lax.optimization_barrier((kept, down))
    across = lax.ppermute(kept, "slab", [(index, index ^ 1) for index in range(32)])
    below = passed_along(down, "slab", -1)
    (copies,) = call(copies_of, [pieces.shape], 1, [SMEM, VMEM, VMEM])(owner, kept, across)
    batches = exchange(copies)
    below, _ = lax.optimization_barrier((below, copies))
    dual, top, side = call(all_duals, [(3,) + block, (ROWS, LANES), (ROWS, LANES)], 4, [VMEM] * 4)(
        field, dual, ahead, below
    )
    before = passed_along(side, "tile", 1)
    above = passed_along(top, "slab", 1)

    (tally,) = call(first_votes, [(BINS + 1, LAYERS + 1, ROWS, LANES)], 4, [SMEM, VMEM])(visible, batches)
    above, before, tally = lax.optimization_barrier((above, before, tally))
    current, extra, side = call(first_update, [block, (LAYERS + 1, ROWS, LANES), (LAYERS, LANES)], 1, [VMEM] * 6)(
        field, dual, above, before, below, tally
    )
    ahead = passed_along(side, "tile", -1)
    (top,) = call(top_dual, [(ROWS, LANES)], 1, [VMEM] * 3)(extra[7:9], dual[:, 7:8], ahead)
    above = passed_along(top, "slab", 1)
    dual, side = call(second_duals, [(3,) + block, (LAYERS, LANES)], 1, [VMEM] * 3 + [ANY])(extra, dual, ahead, top)
    before = passed_along(side, "tile", 1)
    (tally,) = call(second_votes, [(BINS + 1,) + block], 3, [SMEM, VMEM, VMEM, ANY])(visible, batches, tally, side)
    (rest,) = call(last_layers, [block], 1, [VMEM] * 4)(current, dual, before, tally)
    above, rest = lax.optimization_barrier((above, rest))
    (current,) = call(
        last_layer, [block], 1, [first_one, first_one_dual, VMEM, VMEM, tally_one, ANY], grid=(1,),
        out_specs=(first_one,), input_output_aliases={5: 0},
    )(current, dual, above, before, tally, rest)
    return (current, dual)


def solution(mesh):
    placed = (
        P("slab", "tile", None),
        P(None, "slab", "tile", None),
        P("slab", None, None, "tile", None),
        P(),
        P(None, None, "tile"),
    )
    return jax.shard_map(
        per_device,
        mesh=mesh,
        in_specs=placed,
        out_specs=(P("slab", "tile", None), P(None, "slab", "tile", None)),
        check_vma=False,
    )
```

```python
import jax
import jax.numpy as jnp
from jax import lax
from jax.experimental import pallas as pl
from jax.experimental.pallas import tpu as pltpu
from jax.sharding import PartitionSpec as P

VIEWS = 4
BINS = 8
BAND = 6
ITERS = 2

LAYERS = 8
ROWS = 16
LANES = 1024
STEP = 0.1
Z_LAST = 31
X_LAST = 15


def call(kernel, out_shapes, cost_us, in_specs, **more):
    return pl.pallas_call(
        kernel,
        out_shape=tuple(jax.ShapeDtypeStruct(shape, jnp.float32) for shape in out_shapes),
        in_specs=in_specs,
        compiler_params=pltpu.CompilerParams(vmem_limit_bytes=16 << 20),
        cost_estimate=pl.CostEstimate(flops=int(cost_us * 1.0e9), transcendentals=0, bytes_accessed=int(cost_us * 3.0e6)),
        name=kernel.__name__,
        **more,
    )


VMEM = pl.BlockSpec(memory_space=pltpu.VMEM)
SMEM = pl.BlockSpec(memory_space=pltpu.SMEM)
HBM = pl.BlockSpec(memory_space=pltpu.HBM)
ANY = pl.BlockSpec(memory_space=pl.ANY)


def row_ids():
    return lax.broadcasted_iota(jnp.int32, (ROWS, LANES), 0)


def lane_ids():
    return lax.broadcasted_iota(jnp.int32, (ROWS, LANES), 1)


def spread_row(row):
    return jnp.broadcast_to(row, (ROWS, LANES))


def ends():
    row, lane = row_ids(), lane_ids()
    return row, (row == ROWS - 1) & (lax.axis_index("tile") == X_LAST), lane == LANES - 1


def moved_sides(here, ahead_row, dual_x, dual_y):
    row, x_end, y_end = ends()
    ahead_x = jnp.where(row == ROWS - 1, spread_row(ahead_row), pltpu.roll(here, ROWS - 1, 0))
    ahead_y = pltpu.roll(here, LANES - 1, 1)
    moved_x = dual_x + 0.25 * jnp.where(x_end, 0.0, ahead_x - here)
    return moved_x, dual_y + 0.25 * jnp.where(y_end, 0.0, ahead_y - here)


def dual_layer(here, ahead_z, ahead_row, dual_z, dual_x, dual_y, z_end):
    _, x_end, y_end = ends()
    moved_z = dual_z + 0.25 * jnp.where(z_end, 0.0, ahead_z - here)
    moved_x, moved_y = moved_sides(here, ahead_row, dual_x, dual_y)
    norm = moved_z * moved_z + moved_x * moved_x + moved_y * moved_y
    scale = 1.0 / jnp.sqrt(jnp.maximum(norm, 1.0))
    return (
        jnp.where(z_end, 0.0, moved_z * scale),
        jnp.where(x_end, 0.0, moved_x * scale),
        jnp.where(y_end, 0.0, moved_y * scale),
    )


def pick(owner, spread, kept):
    kept[...] = spread[lax.shift_right_logical(owner[lax.shift_right_logical(lax.axis_index("slab"), 4)], 1)]


def copies_of(owner, kept, across, copies):
    slab = lax.axis_index("slab")
    here = (owner[lax.shift_right_logical(slab, 4)] & 1) == (slab & 1)
    piece = jnp.where(here, kept[...], across[...])
    for place in range(16):
        copies[place] = piece


def all_duals(field, dual, ahead, past, new_dual, top, side):
    slab_end = lax.axis_index("slab") == Z_LAST
    for layer in range(LAYERS):
        last = layer == LAYERS - 1
        dual_z, dual_x, dual_y = dual_layer(
            field[layer],
            past[...] if last else field[layer + 1],
            ahead[layer : layer + 1, :],
            dual[0, layer],
            dual[1, layer],
            dual[2, layer],
            slab_end if last else False,
        )
        new_dual[0, layer] = dual_z
        new_dual[1, layer] = dual_x
        new_dual[2, layer] = dual_y
        side[layer : layer + 1, :] = dual_x[15:16, :]
        if last:
            top[...] = dual_z


def second_duals(field, dual, ahead, past, after, new_dual, side):
    slab_end = lax.axis_index("slab") == Z_LAST
    for layer in range(LAYERS):
        last = layer == LAYERS - 1
        dual_z, dual_x, dual_y = dual_layer(
            field[layer],
            past[...] if last else field[layer + 1],
            ahead[layer : layer + 1, :],
            dual[0, layer],
            dual[1, layer],
            dual[2, layer],
            slab_end if last else False,
        )
        new_dual[0, layer] = dual_z
        new_dual[1, layer] = dual_x
        new_dual[2, layer] = dual_y
        side[layer : layer + 1, :] = dual_x[15:16, :]


def flux_of(dual, before, layer):
    row, dual_x, dual_y = spread_row(before[layer : layer + 1, :]), dual[1, layer], dual[2, layer]
    shifted = jnp.where(row_ids() == 0, row, pltpu.roll(dual_x, 1, 0))
    return (dual_x - shifted) + (dual_y - pltpu.roll(dual_y, 1, 1))


def stepped(field, dual, above, before, layer):
    prev = above[...] if layer == 0 else dual[0, layer - 1]
    return field[layer] + 0.25 * ((dual[0, layer] - prev) + flux_of(dual, before, layer))


def first_values(field, dual, before, values):
    values[...] = field[0] + 0.25 * (dual[0, 0] + flux_of(dual, before, 0))


def all_values(field, dual, above, before, values):
    for layer in range(LAYERS):
        values[layer] = stepped(field, dual, above, before, layer)


def ramps(depth, base):
    away = depth - base
    return away * (0.5 * STEP * (BINS - 1) / BAND) + 0.5 * STEP * (BINS - 1), away * (STEP / BAND) + 2.0 * STEP


def votes(views, caps, layer):
    sums, places, weights = None, None, None
    for (place, weight), cap in zip(views, caps):
        q = jnp.clip(place - layer * (0.5 * STEP * (BINS - 1) / BAND), 0.0, STEP * (BINS - 1))
        w = jnp.minimum(jnp.maximum(weight - layer * (STEP / BAND), 0.0), cap)
        e = q + w
        parts = [jnp.maximum(q, jnp.minimum(e, STEP * index)) for index in range(1, BINS)]
        sums = parts if sums is None else [total + part for total, part in zip(sums, parts)]
        places = q if places is None else places + q
        weights = w if weights is None else weights + w
    return sums, places, weights


def proximal(values, sums, places, weights):
    high = values + 0.5 * weights
    best = jnp.maximum(jnp.minimum(high, -1.0), values - 0.5 * weights)
    high = high + places
    for index in range(1, BINS):
        best = jnp.maximum(best, jnp.minimum(high - sums[index - 1], -1.0 + 2.0 * index / (BINS - 1)))
    return best


def block_of(index):
    half, column = index // 8, index % 8
    return half, column, pl.ds(pl.multiple_of(half * 8, 8), 8), pl.ds(pl.multiple_of(column * 128, 128), 128)


def slab_base():
    return (lax.axis_index("slab") * LAYERS).astype(jnp.float32)


def first_votes(visible, batches, tally):
    base = slab_base()
    caps = [STEP * visible[0, view, 0].astype(jnp.float32) for view in range(VIEWS)]

    def body(index, carry):
        half, column, rows, lanes = block_of(index)
        views = [ramps(batches[2 * view + half, column], base) for view in range(VIEWS)]
        for layer in range(LAYERS + 1):
            sums, places, weights = votes(views, caps, float(layer))
            for slot, total in enumerate(sums + [places, weights]):
                tally[slot, layer, rows, lanes] = total
        return carry

    lax.fori_loop(0, 16, body, 0)


def second_votes(visible, batches, tally, after, new_tally):
    base = slab_base()
    caps = [STEP * visible[1, view, 0].astype(jnp.float32) for view in range(VIEWS)]

    def body(index, carry):
        half, column, rows, lanes = block_of(index)
        views = [ramps(batches[2 * (VIEWS + view) + half, column], base) for view in range(VIEWS)]
        for layer in range(LAYERS):
            sums, places, weights = votes(views, caps, float(layer))
            for slot, total in enumerate(sums + [places, weights]):
                new_tally[slot, layer, rows, lanes] = tally[slot, layer, rows, lanes] + total
        return carry

    lax.fori_loop(0, 16, body, 0)


def counted(values, tally, layer):
    sums = [tally[slot, layer] for slot in range(BINS - 1)]
    return proximal(values, sums, tally[BINS - 1, layer], tally[BINS, layer])


def first_update(field, values, tally, updated, extra, side):
    for layer in range(LAYERS):
        new = counted(values[layer], tally, layer)
        updated[layer] = new
        new = 2.0 * new - field[layer]
        extra[layer] = new
        side[layer : layer + 1, :] = new[0:1, :]


def past_update(below, values, dual, tally, extra):
    extra[...] = 2.0 * counted(values[...] - 0.25 * dual[0, 0], tally, 0) - below[...]


def top_dual(extra, past, dual, ahead, top):
    slab_end = lax.axis_index("slab") == Z_LAST
    row = ahead[LAYERS - 1 : LAYERS, :]
    top[...] = dual_layer(extra[0], past[...], row, dual[0, 0], dual[1, 0], dual[2, 0], slab_end)[0]


def last_layers(current, dual, before, tally, updated):
    for layer in range(1, LAYERS):
        updated[layer] = counted(stepped(current, dual, None, before, layer), tally, layer)


def last_layer(current, dual, above, before, tally, updated_in, updated):
    updated[0] = counted(stepped(current, dual, above, before, 0), tally, 0)


def passed_along(value, axis, steps):
    count = lax.axis_size(axis)
    first, last = (max(0, -steps), min(count, count - steps))
    return lax.ppermute(value, axis, [(source, source + steps) for source in range(first, last)])


GROUPS = [[2 * place + half for place in range(16)] for half in range(2)]


def exchange(pieces):
    return lax.all_to_all(pieces, "slab", 0, 0, axis_index_groups=GROUPS)


def per_device(field, dual, depth, owner, visible):
    block = (LAYERS, ROWS, LANES)

    first_one = pl.BlockSpec((1, ROWS, LANES), lambda step: (0, 0, 0))
    first_one_dual = pl.BlockSpec((3, 1, ROWS, LANES), lambda step: (0, 0, 0, 0))
    tally_one = pl.BlockSpec((BINS + 1, 1, ROWS, LANES), lambda step: (0, 0, 0, 0))

    pieces = depth.reshape(16, 8, 8, 128).transpose(0, 2, 1, 3)
    spread = exchange(pieces)

    below = passed_along(field[0], "slab", -1)
    ahead = passed_along(field[:, 0], "tile", -1)
    (kept,) = call(pick, [(8, 8, 128)], 1, [SMEM, VMEM])(owner, spread)
    across = lax.ppermute(kept, "slab", [(index, index ^ 1) for index in range(32)])
    below, ahead, _ = lax.optimization_barrier((below, ahead, kept))
    layer, rows = (ROWS, LANES), (LAYERS, LANES)
    dual, top, side = call(all_duals, [(3,) + block, layer, rows], 1, [VMEM] * 4)(field, dual, ahead, below)
    above = passed_along(top, "slab", 1)
    before = passed_along(side, "tile", 1)
    across, top, side = lax.optimization_barrier((across, top, side))
    (copies,) = call(copies_of, [pieces.shape], 1, [SMEM, VMEM, VMEM])(owner, kept, across)
    batches = exchange(copies)
    (values,) = call(first_values, [layer], 1, [VMEM] * 3)(field, dual, before)
    past_values = passed_along(values, "slab", -1)
    (values,) = call(all_values, [block], 5, [VMEM] * 4)(field, dual, above, before)

    (tally,) = call(first_votes, [(BINS + 1, LAYERS + 1) + layer], 12, [SMEM, VMEM])(visible, batches)
    current, extra, side = call(first_update, [block, block, rows], 1, [VMEM] * 3)(field, values, tally)
    ahead = passed_along(side, "tile", -1)
    last_tally = pl.BlockSpec((BINS + 1, 1) + layer, lambda step: (0, LAYERS, 0, 0))
    last_dual = pl.BlockSpec((3, 1) + layer, lambda step: (0, LAYERS - 1, 0, 0))
    last_block = pl.BlockSpec((1,) + layer, lambda step: (LAYERS - 1, 0, 0))
    past_values, _ = lax.optimization_barrier((past_values, side))
    (past,) = call(past_update, [layer], 1, [VMEM, VMEM, last_dual, last_tally], grid=(1,))(
        below, past_values, dual, tally
    )
    (top,) = call(top_dual, [layer], 1, [last_block, VMEM, last_dual, VMEM], grid=(1,))(extra, past, dual, ahead)
    above = passed_along(top, "slab", 1)
    dual, side = call(second_duals, [(3,) + block, rows], 1, [VMEM] * 4 + [ANY])(extra, dual, ahead, past, top)
    before = passed_along(side, "tile", 1)
    (tally,) = call(second_votes, [(BINS + 1,) + block], 3, [SMEM, VMEM, VMEM, ANY])(visible, batches, tally, side)
    (rest,) = call(last_layers, [block], 1, [VMEM] * 4)(current, dual, before, tally)
    above, rest = lax.optimization_barrier((above, rest))
    (current,) = call(
        last_layer, [block], 1, [first_one, first_one_dual, VMEM, VMEM, tally_one, ANY], grid=(1,),
        out_specs=(first_one,), input_output_aliases={5: 0},
    )(current, dual, above, before, tally, rest)
    return (current, dual)


def solution(mesh):
    placed = (
        P("slab", "tile", None),
        P(None, "slab", "tile", None),
        P("slab", None, None, "tile", None),
        P(),
        P(None, None, "tile"),
    )
    return jax.shard_map(
        per_device,
        mesh=mesh,
        in_specs=placed,
        out_specs=(P("slab", "tile", None), P(None, "slab", "tile", None)),
        check_vma=False,
    )
```

```python
import jax
import jax.numpy as jnp
from jax import lax
from jax.experimental import pallas as pl
from jax.experimental.pallas import tpu as pltpu
from jax.sharding import PartitionSpec as P

VIEWS = 4
BINS = 8
BAND = 6
ITERS = 2

LAYERS = 8
ROWS = 16
LANES = 1024
STEP = 0.1
Z_LAST = 31
X_LAST = 15


def call(kernel, out_shapes, cost_us, in_specs, **more):
    return pl.pallas_call(
        kernel,
        out_shape=tuple(jax.ShapeDtypeStruct(shape, jnp.float32) for shape in out_shapes),
        in_specs=in_specs,
        compiler_params=pltpu.CompilerParams(vmem_limit_bytes=16 << 20),
        cost_estimate=pl.CostEstimate(flops=int(cost_us * 1.0e9), transcendentals=0, bytes_accessed=int(cost_us * 3.0e6)),
        name=kernel.__name__,
        **more,
    )


VMEM = pl.BlockSpec(memory_space=pltpu.VMEM)
SMEM = pl.BlockSpec(memory_space=pltpu.SMEM)
HBM = pl.BlockSpec(memory_space=pltpu.HBM)
ANY = pl.BlockSpec(memory_space=pl.ANY)


def row_ids():
    return lax.broadcasted_iota(jnp.int32, (ROWS, LANES), 0)


def lane_ids():
    return lax.broadcasted_iota(jnp.int32, (ROWS, LANES), 1)


def spread_row(row):
    return jnp.broadcast_to(row, (ROWS, LANES))


def ends():
    row, lane = row_ids(), lane_ids()
    return row, (row == ROWS - 1) & (lax.axis_index("tile") == X_LAST), lane == LANES - 1


def moved_sides(here, ahead_row, dual_x, dual_y):
    row, x_end, y_end = ends()
    ahead_x = jnp.where(row == ROWS - 1, spread_row(ahead_row), pltpu.roll(here, ROWS - 1, 0))
    ahead_y = pltpu.roll(here, LANES - 1, 1)
    moved_x = dual_x + 0.25 * jnp.where(x_end, 0.0, ahead_x - here)
    return moved_x, dual_y + 0.25 * jnp.where(y_end, 0.0, ahead_y - here)


def dual_layer(here, ahead_z, ahead_row, dual_z, dual_x, dual_y, z_end):
    _, x_end, y_end = ends()
    moved_z = dual_z + 0.25 * jnp.where(z_end, 0.0, ahead_z - here)
    moved_x, moved_y = moved_sides(here, ahead_row, dual_x, dual_y)
    norm = moved_z * moved_z + moved_x * moved_x + moved_y * moved_y
    scale = 1.0 / jnp.sqrt(jnp.maximum(norm, 1.0))
    return (
        jnp.where(z_end, 0.0, moved_z * scale),
        jnp.where(x_end, 0.0, moved_x * scale),
        jnp.where(y_end, 0.0, moved_y * scale),
    )


def pick(owner, spread, kept):
    kept[...] = spread[lax.shift_right_logical(owner[lax.shift_right_logical(lax.axis_index("slab"), 4)], 1)]


def copies_of(owner, kept, across, copies, piece, sems):
    slab = lax.axis_index("slab")
    here = (owner[lax.shift_right_logical(slab, 4)] & 1) == (slab & 1)
    piece[...] = jnp.where(here, kept[...], across[...])
    moves = [pltpu.make_async_copy(piece, copies.at[place], sems.at[place]) for place in range(16)]
    for move in moves:
        move.start()
    for move in moves:
        move.wait()


def all_duals(field, dual, ahead, past, new_dual, top, side):
    slab_end = lax.axis_index("slab") == Z_LAST
    for layer in range(LAYERS):
        last = layer == LAYERS - 1
        dual_z, dual_x, dual_y = dual_layer(
            field[layer],
            past[...] if last else field[layer + 1],
            ahead[layer : layer + 1, :],
            dual[0, layer],
            dual[1, layer],
            dual[2, layer],
            slab_end if last else False,
        )
        new_dual[0, layer] = dual_z
        new_dual[1, layer] = dual_x
        new_dual[2, layer] = dual_y
        side[layer : layer + 1, :] = dual_x[15:16, :]
        if last:
            top[...] = dual_z


def second_duals(field, dual, ahead, past, after, new_dual, side):
    slab_end = lax.axis_index("slab") == Z_LAST
    for layer in range(LAYERS):
        last = layer == LAYERS - 1
        dual_z, dual_x, dual_y = dual_layer(
            field[layer],
            past[...] if last else field[layer + 1],
            ahead[layer : layer + 1, :],
            dual[0, layer],
            dual[1, layer],
            dual[2, layer],
            slab_end if last else False,
        )
        new_dual[0, layer] = dual_z
        new_dual[1, layer] = dual_x
        new_dual[2, layer] = dual_y
        side[layer : layer + 1, :] = dual_x[15:16, :]


def flux_of(dual, before, layer):
    row, dual_x, dual_y = spread_row(before[layer : layer + 1, :]), dual[1, layer], dual[2, layer]
    shifted = jnp.where(row_ids() == 0, row, pltpu.roll(dual_x, 1, 0))
    return (dual_x - shifted) + (dual_y - pltpu.roll(dual_y, 1, 1))


def stepped(field, dual, above, before, layer):
    prev = above[...] if layer == 0 else dual[0, layer - 1]
    return field[layer] + 0.25 * ((dual[0, layer] - prev) + flux_of(dual, before, layer))


def first_values(field, dual, before, values):
    values[...] = field[0] + 0.25 * (dual[0, 0] + flux_of(dual, before, 0))


def all_values(field, dual, above, before, values):
    for layer in range(LAYERS):
        values[layer] = stepped(field, dual, above, before, layer)


def ramps(depth, base):
    away = depth - base
    return away * (0.5 * STEP * (BINS - 1) / BAND) + 0.5 * STEP * (BINS - 1), away * (STEP / BAND) + 2.0 * STEP


def votes(views, caps, layer):
    sums, places, weights = None, None, None
    for (place, weight), cap in zip(views, caps):
        q = jnp.clip(place - layer * (0.5 * STEP * (BINS - 1) / BAND), 0.0, STEP * (BINS - 1))
        w = jnp.minimum(jnp.maximum(weight - layer * (STEP / BAND), 0.0), cap)
        e = q + w
        parts = [jnp.maximum(q, jnp.minimum(e, STEP * index)) for index in range(1, BINS)]
        sums = parts if sums is None else [total + part for total, part in zip(sums, parts)]
        places = q if places is None else places + q
        weights = w if weights is None else weights + w
    return sums, places, weights


def proximal(values, sums, places, weights):
    high = values + 0.5 * weights
    best = jnp.maximum(jnp.minimum(high, -1.0), values - 0.5 * weights)
    high = high + places
    for index in range(1, BINS):
        best = jnp.maximum(best, jnp.minimum(high - sums[index - 1], -1.0 + 2.0 * index / (BINS - 1)))
    return best


def block_of(index):
    half, column = index // 8, index % 8
    return half, column, pl.ds(pl.multiple_of(half * 8, 8), 8), pl.ds(pl.multiple_of(column * 128, 128), 128)


def slab_base():
    return (lax.axis_index("slab") * LAYERS).astype(jnp.float32)


def first_votes(visible, batches, tally):
    base = slab_base()
    caps = [STEP * visible[0, 0, view].astype(jnp.float32) for view in range(VIEWS)]

    def body(index, carry):
        half, column, rows, lanes = block_of(index)
        views = [ramps(batches[2 * view + half, column], base) for view in range(VIEWS)]
        for layer in range(LAYERS + 1):
            sums, places, weights = votes(views, caps, float(layer))
            for slot, total in enumerate(sums + [places, weights]):
                tally[slot, layer, rows, lanes] = total
        return carry

    lax.fori_loop(0, 16, body, 0)


def second_votes(visible, batches, tally, after, new_tally):
    base = slab_base()
    caps = [STEP * visible[1, 0, view].astype(jnp.float32) for view in range(VIEWS)]

    def body(index, carry):
        half, column, rows, lanes = block_of(index)
        views = [ramps(batches[2 * (VIEWS + view) + half, column], base) for view in range(VIEWS)]
        for layer in range(LAYERS):
            sums, places, weights = votes(views, caps, float(layer))
            for slot, total in enumerate(sums + [places, weights]):
                new_tally[slot, layer, rows, lanes] = tally[slot, layer, rows, lanes] + total
        return carry

    lax.fori_loop(0, 16, body, 0)


def counted(values, tally, layer):
    sums = [tally[slot, layer] for slot in range(BINS - 1)]
    return proximal(values, sums, tally[BINS - 1, layer], tally[BINS, layer])


def first_update(field, values, tally, updated, extra, side):
    for layer in range(LAYERS):
        new = counted(values[layer], tally, layer)
        updated[layer] = new
        new = 2.0 * new - field[layer]
        extra[layer] = new
        side[layer : layer + 1, :] = new[0:1, :]


def past_update(below, values, dual, tally, extra):
    extra[...] = 2.0 * counted(values[...] - 0.25 * dual[0, 0], tally, 0) - below[...]


def top_dual(extra, past, dual, ahead, top):
    slab_end = lax.axis_index("slab") == Z_LAST
    row = ahead[LAYERS - 1 : LAYERS, :]
    top[...] = dual_layer(extra[0], past[...], row, dual[0, 0], dual[1, 0], dual[2, 0], slab_end)[0]


def last_layers(current, dual, before, tally, updated):
    for layer in range(1, LAYERS):
        updated[layer] = counted(stepped(current, dual, None, before, layer), tally, layer)


def last_layer(current, dual, above, before, tally, updated_in, updated):
    updated[0] = counted(stepped(current, dual, above, before, 0), tally, 0)


def passed_along(value, axis, steps):
    count = lax.axis_size(axis)
    first, last = (max(0, -steps), min(count, count - steps))
    return lax.ppermute(value, axis, [(source, source + steps) for source in range(first, last)])


GROUPS = [[2 * place + half for place in range(16)] for half in range(2)]


def exchange(pieces):
    return lax.all_to_all(pieces, "slab", 0, 0, axis_index_groups=GROUPS)


def per_device(field, dual, depth, owner, visible):
    block = (LAYERS, ROWS, LANES)
    owner = pltpu.with_memory_space_constraint(owner, pltpu.HBM)
    visible = visible.transpose(0, 2, 1)

    first_one = pl.BlockSpec((1, ROWS, LANES), lambda step: (0, 0, 0))
    first_one_dual = pl.BlockSpec((3, 1, ROWS, LANES), lambda step: (0, 0, 0, 0))
    tally_one = pl.BlockSpec((BINS + 1, 1, ROWS, LANES), lambda step: (0, 0, 0, 0))

    pieces = depth.reshape(16, 8, 8, 128).transpose(0, 2, 1, 3)
    spread = exchange(pieces)

    below = passed_along(field[0], "slab", -1)
    (kept,) = call(pick, [(8, 8, 128)], 1, [SMEM, VMEM])(owner, spread)
    first_rows, _ = lax.optimization_barrier((field[:, 0], kept))
    ahead = passed_along(first_rows, "tile", -1)
    across = lax.ppermute(kept, "slab", [(index, index ^ 1) for index in range(32)])
    across, below = lax.optimization_barrier((across, below))
    (copies,) = call(
        copies_of, [pieces.shape], 1, [SMEM, VMEM, VMEM], out_specs=(ANY,),
        scratch_shapes=[pltpu.VMEM((8, 8, 128), jnp.float32), pltpu.SemaphoreType.DMA((16,))],
    )(owner, kept, across)
    ahead, _ = lax.optimization_barrier((ahead, copies))
    layer, rows = (ROWS, LANES), (LAYERS, LANES)
    dual, top, side = call(all_duals, [(3,) + block, layer, rows], 1, [VMEM] * 4)(field, dual, ahead, below)
    above = passed_along(top, "slab", 1)
    before = passed_along(side, "tile", 1)
    batches = exchange(copies)
    (values,) = call(first_values, [layer], 1, [VMEM] * 3)(field, dual, before)
    past_values = passed_along(values, "slab", -1)
    (values,) = call(all_values, [block], 5, [VMEM] * 4)(field, dual, above, before)

    (tally,) = call(first_votes, [(BINS + 1, LAYERS + 1) + layer], 12, [SMEM, VMEM])(visible, batches)
    current, extra, side = call(first_update, [block, block, rows], 1, [VMEM] * 3)(field, values, tally)
    ahead = passed_along(side, "tile", -1)
    last_tally = pl.BlockSpec((BINS + 1, 1) + layer, lambda step: (0, LAYERS, 0, 0))
    last_dual = pl.BlockSpec((3, 1) + layer, lambda step: (0, LAYERS - 1, 0, 0))
    last_block = pl.BlockSpec((1,) + layer, lambda step: (LAYERS - 1, 0, 0))
    past_values, _ = lax.optimization_barrier((past_values, side))
    (past,) = call(past_update, [layer], 1, [VMEM, VMEM, last_dual, last_tally], grid=(1,))(
        below, past_values, dual, tally
    )
    (top,) = call(top_dual, [layer], 1, [last_block, VMEM, last_dual, VMEM], grid=(1,))(extra, past, dual, ahead)
    above = passed_along(top, "slab", 1)
    dual, side = call(second_duals, [(3,) + block, rows], 1, [VMEM] * 4 + [ANY])(extra, dual, ahead, past, top)
    before = passed_along(side, "tile", 1)
    (tally,) = call(second_votes, [(BINS + 1,) + block], 3, [SMEM, VMEM, VMEM, ANY])(visible, batches, tally, side)
    (rest,) = call(last_layers, [block], 1, [VMEM] * 4)(current, dual, before, tally)
    above, rest = lax.optimization_barrier((above, rest))
    (current,) = call(
        last_layer, [block], 1, [first_one, first_one_dual, VMEM, VMEM, tally_one, ANY], grid=(1,),
        out_specs=(first_one,), input_output_aliases={5: 0},
    )(current, dual, above, before, tally, rest)
    return (current, dual)


def solution(mesh):
    placed = (
        P("slab", "tile", None),
        P(None, "slab", "tile", None),
        P("slab", None, None, "tile", None),
        P(),
        P(None, None, "tile"),
    )
    return jax.shard_map(
        per_device,
        mesh=mesh,
        in_specs=placed,
        out_specs=(P("slab", "tile", None), P(None, "slab", "tile", None)),
        check_vma=False,
    )
```

```python
import jax
import jax.numpy as jnp
from jax import lax
from jax.experimental import pallas as pl
from jax.experimental.pallas import tpu as pltpu
from jax.sharding import PartitionSpec as P

VIEWS = 4
BINS = 8
BAND = 6
ITERS = 2

LAYERS = 8
ROWS = 16
LANES = 1024
STEP = 0.1
Z_LAST = 31
X_LAST = 15


def call(kernel, out_shapes, cost_us, in_specs, **more):
    return pl.pallas_call(
        kernel,
        out_shape=tuple(jax.ShapeDtypeStruct(shape, jnp.float32) for shape in out_shapes),
        in_specs=in_specs,
        compiler_params=pltpu.CompilerParams(vmem_limit_bytes=16 << 20),
        cost_estimate=pl.CostEstimate(flops=int(cost_us * 1.0e9), transcendentals=0, bytes_accessed=int(cost_us * 3.0e6)),
        name=kernel.__name__,
        **more,
    )


VMEM = pl.BlockSpec(memory_space=pltpu.VMEM)
SMEM = pl.BlockSpec(memory_space=pltpu.SMEM)
HBM = pl.BlockSpec(memory_space=pltpu.HBM)
ANY = pl.BlockSpec(memory_space=pl.ANY)


def row_ids():
    return lax.broadcasted_iota(jnp.int32, (ROWS, LANES), 0)


def lane_ids():
    return lax.broadcasted_iota(jnp.int32, (ROWS, LANES), 1)


def spread_row(row):
    return jnp.broadcast_to(row, (ROWS, LANES))


def ends():
    row, lane = row_ids(), lane_ids()
    return row, (row == ROWS - 1) & (lax.axis_index("tile") == X_LAST), lane == LANES - 1


def moved_sides(here, ahead_row, dual_x, dual_y):
    row, x_end, y_end = ends()
    ahead_x = jnp.where(row == ROWS - 1, spread_row(ahead_row), pltpu.roll(here, ROWS - 1, 0))
    ahead_y = pltpu.roll(here, LANES - 1, 1)
    moved_x = dual_x + 0.25 * jnp.where(x_end, 0.0, ahead_x - here)
    return moved_x, dual_y + 0.25 * jnp.where(y_end, 0.0, ahead_y - here)


def dual_layer(here, ahead_z, ahead_row, dual_z, dual_x, dual_y, z_end):
    _, x_end, y_end = ends()
    moved_z = dual_z + 0.25 * jnp.where(z_end, 0.0, ahead_z - here)
    moved_x, moved_y = moved_sides(here, ahead_row, dual_x, dual_y)
    norm = moved_z * moved_z + moved_x * moved_x + moved_y * moved_y
    scale = 1.0 / jnp.sqrt(jnp.maximum(norm, 1.0))
    return (
        jnp.where(z_end, 0.0, moved_z * scale),
        jnp.where(x_end, 0.0, moved_x * scale),
        jnp.where(y_end, 0.0, moved_y * scale),
    )


def pick(owner, spread, kept):
    kept[...] = spread[lax.shift_right_logical(owner[lax.shift_right_logical(lax.axis_index("slab"), 4)], 1)]


def copies_of(owner, kept, across, copies, piece, sems):
    slab = lax.axis_index("slab")
    here = (owner[lax.shift_right_logical(slab, 4)] & 1) == (slab & 1)
    piece[...] = jnp.where(here, kept[...], across[...])
    moves = [pltpu.make_async_copy(piece, copies.at[place], sems.at[place]) for place in range(16)]
    for move in moves:
        move.start()
    for move in moves:
        move.wait()


def staged(field, first_layer, first_rows, field_here, sems):
    moves = [
        pltpu.make_async_copy(field.at[:, 0], first_rows, sems.at[0]),
        pltpu.make_async_copy(field.at[0], first_layer, sems.at[1]),
        pltpu.make_async_copy(field, field_here, sems.at[2]),
    ]
    for move in moves:
        move.start()
    for move in moves:
        move.wait()


def all_duals(field, given, ahead, past, new_dual, top, side, dual, sems):
    moves = [pltpu.make_async_copy(given.at[:, layer], dual.at[layer], sems.at[layer]) for layer in range(LAYERS)]
    for move in moves:
        move.start()
    slab_end = lax.axis_index("slab") == Z_LAST
    for layer in range(LAYERS):
        last = layer == LAYERS - 1
        moves[layer].wait()
        dual_z, dual_x, dual_y = dual_layer(
            field[layer],
            past[...] if last else field[layer + 1],
            ahead[layer : layer + 1, :],
            dual[layer, 0],
            dual[layer, 1],
            dual[layer, 2],
            slab_end if last else False,
        )
        new_dual[0, layer] = dual_z
        new_dual[1, layer] = dual_x
        new_dual[2, layer] = dual_y
        side[layer : layer + 1, :] = dual_x[15:16, :]
        if last:
            top[...] = dual_z


def second_duals(field, dual, ahead, past, after, new_dual, side):
    slab_end = lax.axis_index("slab") == Z_LAST
    for layer in range(LAYERS):
        last = layer == LAYERS - 1
        dual_z, dual_x, dual_y = dual_layer(
            field[layer],
            past[...] if last else field[layer + 1],
            ahead[layer : layer + 1, :],
            dual[0, layer],
            dual[1, layer],
            dual[2, layer],
            slab_end if last else False,
        )
        new_dual[0, layer] = dual_z
        new_dual[1, layer] = dual_x
        new_dual[2, layer] = dual_y
        side[layer : layer + 1, :] = dual_x[15:16, :]


def flux_of(dual, before, layer):
    row, dual_x, dual_y = spread_row(before[layer : layer + 1, :]), dual[1, layer], dual[2, layer]
    shifted = jnp.where(row_ids() == 0, row, pltpu.roll(dual_x, 1, 0))
    return (dual_x - shifted) + (dual_y - pltpu.roll(dual_y, 1, 1))


def stepped(field, dual, above, before, layer):
    prev = above[...] if layer == 0 else dual[0, layer - 1]
    return field[layer] + 0.25 * ((dual[0, layer] - prev) + flux_of(dual, before, layer))


def first_values(field, dual, before, values):
    values[...] = field[0] + 0.25 * (dual[0, 0] + flux_of(dual, before, 0))


def all_values(field, dual, above, before, values):
    for layer in range(LAYERS):
        values[layer] = stepped(field, dual, above, before, layer)


def ramps(depth, base):
    away = depth - base
    return away * (0.5 * STEP * (BINS - 1) / BAND) + 0.5 * STEP * (BINS - 1), away * (STEP / BAND) + 2.0 * STEP


def votes(views, caps, layer):
    sums, places, weights = None, None, None
    for (place, weight), cap in zip(views, caps):
        q = jnp.clip(place - layer * (0.5 * STEP * (BINS - 1) / BAND), 0.0, STEP * (BINS - 1))
        w = jnp.minimum(jnp.maximum(weight - layer * (STEP / BAND), 0.0), cap)
        e = q + w
        parts = [jnp.maximum(q, jnp.minimum(e, STEP * index)) for index in range(1, BINS)]
        sums = parts if sums is None else [total + part for total, part in zip(sums, parts)]
        places = q if places is None else places + q
        weights = w if weights is None else weights + w
    return sums, places, weights


def proximal(values, sums, places, weights):
    high = values + 0.5 * weights
    best = jnp.maximum(jnp.minimum(high, -1.0), values - 0.5 * weights)
    high = high + places
    for index in range(1, BINS):
        best = jnp.maximum(best, jnp.minimum(high - sums[index - 1], -1.0 + 2.0 * index / (BINS - 1)))
    return best


def block_of(index):
    half, column = index // 8, index % 8
    return half, column, pl.ds(pl.multiple_of(half * 8, 8), 8), pl.ds(pl.multiple_of(column * 128, 128), 128)


def slab_base():
    return (lax.axis_index("slab") * LAYERS).astype(jnp.float32)


def first_votes(visible, batches, tally):
    base = slab_base()
    caps = [STEP * visible[0, 0, view].astype(jnp.float32) for view in range(VIEWS)]

    def body(index, carry):
        half, column, rows, lanes = block_of(index)
        views = [ramps(batches[2 * view + half, column], base) for view in range(VIEWS)]
        for layer in range(LAYERS + 1):
            sums, places, weights = votes(views, caps, float(layer))
            for slot, total in enumerate(sums + [places, weights]):
                tally[slot, layer, rows, lanes] = total
        return carry

    lax.fori_loop(0, 16, body, 0)


def second_votes(visible, batches, tally, after, new_tally):
    base = slab_base()
    caps = [STEP * visible[1, 0, view].astype(jnp.float32) for view in range(VIEWS)]

    def body(index, carry):
        half, column, rows, lanes = block_of(index)
        views = [ramps(batches[2 * (VIEWS + view) + half, column], base) for view in range(VIEWS)]
        for layer in range(LAYERS):
            sums, places, weights = votes(views, caps, float(layer))
            for slot, total in enumerate(sums + [places, weights]):
                new_tally[slot, layer, rows, lanes] = tally[slot, layer, rows, lanes] + total
        return carry

    lax.fori_loop(0, 16, body, 0)


def counted(values, tally, layer):
    sums = [tally[slot, layer] for slot in range(BINS - 1)]
    return proximal(values, sums, tally[BINS - 1, layer], tally[BINS, layer])


def first_update(field, values, tally, updated, extra, side):
    for layer in range(LAYERS):
        new = counted(values[layer], tally, layer)
        updated[layer] = new
        new = 2.0 * new - field[layer]
        extra[layer] = new
        side[layer : layer + 1, :] = new[0:1, :]


def past_update(below, values, dual, tally, extra):
    extra[...] = 2.0 * counted(values[...] - 0.25 * dual[0, LAYERS - 1], tally, LAYERS) - below[...]


def top_dual(extra, past, dual, ahead, top):
    last = LAYERS - 1
    slab_end = lax.axis_index("slab") == Z_LAST
    row = ahead[last:LAYERS, :]
    top[...] = dual_layer(extra[last], past[...], row, dual[0, last], dual[1, last], dual[2, last], slab_end)[0]


def last_layers(current, dual, before, tally, updated):
    for layer in range(1, LAYERS):
        updated[layer] = counted(stepped(current, dual, None, before, layer), tally, layer)


def last_layer(current, dual, above, before, tally, updated_in, updated, layer, sem):
    layer[...] = counted(stepped(current, dual, above, before, 0), tally, 0)
    move = pltpu.make_async_copy(layer, updated.at[0], sem)
    move.start()
    move.wait()


def passed_along(value, axis, steps):
    count = lax.axis_size(axis)
    first, last = (max(0, -steps), min(count, count - steps))
    return lax.ppermute(value, axis, [(source, source + steps) for source in range(first, last)])


GROUPS = [[2 * place + half for place in range(16)] for half in range(2)]


def exchange(pieces):
    return lax.all_to_all(pieces, "slab", 0, 0, axis_index_groups=GROUPS)


def per_device(field, dual, depth, owner, visible):
    block = (LAYERS, ROWS, LANES)
    owner = pltpu.with_memory_space_constraint(owner, pltpu.HBM)
    visible = visible.transpose(0, 2, 1)

    pieces = depth.reshape(16, 8, 8, 128).transpose(0, 2, 1, 3)
    spread = exchange(pieces)

    first_layer, first_rows, field = call(
        staged, [(ROWS, LANES), (LAYERS, LANES), block], 1, [HBM], scratch_shapes=[pltpu.SemaphoreType.DMA((3,))]
    )(pltpu.with_memory_space_constraint(field, pltpu.HBM))
    below = passed_along(first_layer, "slab", -1)
    ahead = passed_along(first_rows, "tile", -1)
    (kept,) = call(pick, [(8, 8, 128)], 1, [SMEM, VMEM])(owner, spread)
    across = lax.ppermute(kept, "slab", [(index, index ^ 1) for index in range(32)])
    below, ahead, _ = lax.optimization_barrier((below, ahead, kept))
    layer, rows = (ROWS, LANES), (LAYERS, LANES)
    dual, top, side = call(
        all_duals, [(3,) + block, layer, rows], 1, [VMEM, HBM, VMEM, VMEM],
        scratch_shapes=[pltpu.VMEM((LAYERS, 3, ROWS, LANES), jnp.float32), pltpu.SemaphoreType.DMA((LAYERS,))],
    )(field, pltpu.with_memory_space_constraint(dual, pltpu.HBM), ahead, below)
    above = passed_along(top, "slab", 1)
    before = passed_along(side, "tile", 1)
    across, top, side = lax.optimization_barrier((across, top, side))
    (copies,) = call(
        copies_of, [pieces.shape], 1, [SMEM, VMEM, VMEM], out_specs=(ANY,),
        scratch_shapes=[pltpu.VMEM((8, 8, 128), jnp.float32), pltpu.SemaphoreType.DMA((16,))],
    )(owner, kept, across)
    batches = exchange(copies)
    (values,) = call(first_values, [layer], 1, [VMEM] * 3)(field, dual, before)
    past_values = passed_along(values, "slab", -1)
    (values,) = call(all_values, [block], 5, [VMEM] * 4)(field, dual, above, before)

    (tally,) = call(first_votes, [(BINS + 1, LAYERS + 1) + layer], 12, [SMEM, VMEM])(visible, batches)
    current, extra, side = call(first_update, [block, block, rows], 1, [VMEM] * 3)(field, values, tally)
    ahead = passed_along(side, "tile", -1)
    past_values, _ = lax.optimization_barrier((past_values, side))
    (past,) = call(past_update, [layer], 1, [VMEM] * 4)(below, past_values, dual, tally)
    (top,) = call(top_dual, [layer], 1, [VMEM] * 4)(extra, past, dual, ahead)
    above = passed_along(top, "slab", 1)
    dual, side = call(second_duals, [(3,) + block, rows], 1, [VMEM] * 4 + [ANY])(extra, dual, ahead, past, top)
    before = passed_along(side, "tile", 1)
    (tally,) = call(second_votes, [(BINS + 1,) + block], 3, [SMEM, VMEM, VMEM, ANY])(visible, batches, tally, side)
    (rest,) = call(last_layers, [block], 1, [VMEM] * 4)(current, dual, before, tally)
    above, rest = lax.optimization_barrier((above, rest))
    (current,) = call(
        last_layer, [block], 1, [VMEM] * 5 + [ANY], out_specs=(ANY,), input_output_aliases={5: 0},
        scratch_shapes=[pltpu.VMEM((ROWS, LANES), jnp.float32), pltpu.SemaphoreType.DMA],
    )(current, dual, above, before, tally, rest)
    return (current, dual)


def solution(mesh):
    placed = (
        P("slab", "tile", None),
        P(None, "slab", "tile", None),
        P("slab", None, None, "tile", None),
        P(),
        P(None, None, "tile"),
    )
    return jax.shard_map(
        per_device,
        mesh=mesh,
        in_specs=placed,
        out_specs=(P("slab", "tile", None), P(None, "slab", "tile", None)),
        check_vma=False,
    )
```

```python
import jax
import jax.numpy as jnp
from jax import lax
from jax.experimental import pallas as pl
from jax.experimental.pallas import tpu as pltpu
from jax.sharding import PartitionSpec as P

VIEWS = 4
BINS = 8
BAND = 6
ITERS = 2

LAYERS = 8
ROWS = 16
LANES = 1024
STEP = 0.1
Z_LAST = 31
X_LAST = 15


def call(kernel, out_shapes, cost_us, in_specs, **more):
    return pl.pallas_call(
        kernel,
        out_shape=tuple(jax.ShapeDtypeStruct(shape, jnp.float32) for shape in out_shapes),
        in_specs=in_specs,
        compiler_params=pltpu.CompilerParams(vmem_limit_bytes=16 << 20),
        cost_estimate=pl.CostEstimate(flops=int(cost_us * 1.0e9), transcendentals=0, bytes_accessed=int(cost_us * 3.0e6)),
        name=kernel.__name__,
        **more,
    )


VMEM = pl.BlockSpec(memory_space=pltpu.VMEM)
SMEM = pl.BlockSpec(memory_space=pltpu.SMEM)
HBM = pl.BlockSpec(memory_space=pltpu.HBM)
ANY = pl.BlockSpec(memory_space=pl.ANY)


def row_ids():
    return lax.broadcasted_iota(jnp.int32, (ROWS, LANES), 0)


def lane_ids():
    return lax.broadcasted_iota(jnp.int32, (ROWS, LANES), 1)


def spread_row(row):
    return jnp.broadcast_to(row, (ROWS, LANES))


def ends():
    row, lane = row_ids(), lane_ids()
    return row, (row == ROWS - 1) & (lax.axis_index("tile") == X_LAST), lane == LANES - 1


def moved_sides(here, ahead_row, dual_x, dual_y):
    row, x_end, y_end = ends()
    ahead_x = jnp.where(row == ROWS - 1, spread_row(ahead_row), pltpu.roll(here, ROWS - 1, 0))
    ahead_y = pltpu.roll(here, LANES - 1, 1)
    moved_x = dual_x + 0.25 * jnp.where(x_end, 0.0, ahead_x - here)
    return moved_x, dual_y + 0.25 * jnp.where(y_end, 0.0, ahead_y - here)


def dual_layer(here, ahead_z, ahead_row, dual_z, dual_x, dual_y, z_end):
    _, x_end, y_end = ends()
    moved_z = dual_z + 0.25 * jnp.where(z_end, 0.0, ahead_z - here)
    moved_x, moved_y = moved_sides(here, ahead_row, dual_x, dual_y)
    norm = moved_z * moved_z + moved_x * moved_x + moved_y * moved_y
    scale = 1.0 / jnp.sqrt(jnp.maximum(norm, 1.0))
    return (
        jnp.where(z_end, 0.0, moved_z * scale),
        jnp.where(x_end, 0.0, moved_x * scale),
        jnp.where(y_end, 0.0, moved_y * scale),
    )


def pick(owner, spread, kept):
    kept[...] = spread[lax.shift_right_logical(owner[lax.shift_right_logical(lax.axis_index("slab"), 4)], 1)]


def copies_of(owner, kept, across, copies):
    slab = lax.axis_index("slab")
    here = (owner[lax.shift_right_logical(slab, 4)] & 1) == (slab & 1)
    piece = jnp.where(here, kept[...], across[...])
    for place in range(16):
        copies[place] = piece


def staged(field, first_layer, first_rows, field_here, sems):
    moves = [
        pltpu.make_async_copy(field.at[:, 0], first_rows, sems.at[0]),
        pltpu.make_async_copy(field.at[0], first_layer, sems.at[1]),
        pltpu.make_async_copy(field, field_here, sems.at[2]),
    ]
    for move in moves:
        move.start()
    for move in moves:
        move.wait()


def relay(given, same):
    same[...] = given[...]


def all_duals(field, dual, ahead, past, new_dual, top, side):
    slab_end = lax.axis_index("slab") == Z_LAST
    for layer in range(LAYERS):
        last = layer == LAYERS - 1
        dual_z, dual_x, dual_y = dual_layer(
            field[layer],
            past[...] if last else field[layer + 1],
            ahead[layer : layer + 1, :],
            dual[0, layer],
            dual[1, layer],
            dual[2, layer],
            slab_end if last else False,
        )
        new_dual[0, layer] = dual_z
        new_dual[1, layer] = dual_x
        new_dual[2, layer] = dual_y
        side[layer : layer + 1, :] = dual_x[15:16, :]
        if last:
            top[...] = dual_z


def second_duals(field, dual, ahead, past, after, new_dual, side):
    slab_end = lax.axis_index("slab") == Z_LAST
    for layer in range(LAYERS):
        last = layer == LAYERS - 1
        dual_z, dual_x, dual_y = dual_layer(
            field[layer],
            past[...] if last else field[layer + 1],
            ahead[layer : layer + 1, :],
            dual[0, layer],
            dual[1, layer],
            dual[2, layer],
            slab_end if last else False,
        )
        new_dual[0, layer] = dual_z
        new_dual[1, layer] = dual_x
        new_dual[2, layer] = dual_y
        side[layer : layer + 1, :] = dual_x[15:16, :]


def flux_of(dual, before, layer):
    row, dual_x, dual_y = spread_row(before[layer : layer + 1, :]), dual[1, layer], dual[2, layer]
    shifted = jnp.where(row_ids() == 0, row, pltpu.roll(dual_x, 1, 0))
    return (dual_x - shifted) + (dual_y - pltpu.roll(dual_y, 1, 1))


def stepped(field, dual, above, before, layer):
    prev = above[...] if layer == 0 else dual[0, layer - 1]
    return field[layer] + 0.25 * ((dual[0, layer] - prev) + flux_of(dual, before, layer))


def first_values(field, dual, before, values):
    values[...] = field[0] + 0.25 * (dual[0, 0] + flux_of(dual, before, 0))


def all_values(field, dual, above, before, values):
    for layer in range(LAYERS):
        values[layer] = stepped(field, dual, above, before, layer)


def ramps(depth, base):
    away = depth - base
    return away * (0.5 * STEP * (BINS - 1) / BAND) + 0.5 * STEP * (BINS - 1), away * (STEP / BAND) + 2.0 * STEP


def votes(views, caps, layer):
    sums, places, weights = None, None, None
    for (place, weight), cap in zip(views, caps):
        q = jnp.clip(place - layer * (0.5 * STEP * (BINS - 1) / BAND), 0.0, STEP * (BINS - 1))
        w = jnp.minimum(jnp.maximum(weight - layer * (STEP / BAND), 0.0), cap)
        e = q + w
        parts = [jnp.maximum(q, jnp.minimum(e, STEP * index)) for index in range(1, BINS)]
        sums = parts if sums is None else [total + part for total, part in zip(sums, parts)]
        places = q if places is None else places + q
        weights = w if weights is None else weights + w
    return sums, places, weights


def proximal(values, sums, places, weights):
    high = values + 0.5 * weights
    best = jnp.maximum(jnp.minimum(high, -1.0), values - 0.5 * weights)
    high = high + places
    for index in range(1, BINS):
        best = jnp.maximum(best, jnp.minimum(high - sums[index - 1], -1.0 + 2.0 * index / (BINS - 1)))
    return best


def block_of(index):
    half, column = index // 8, index % 8
    return half, column, pl.ds(pl.multiple_of(half * 8, 8), 8), pl.ds(pl.multiple_of(column * 128, 128), 128)


def slab_base():
    return (lax.axis_index("slab") * LAYERS).astype(jnp.float32)


def first_votes(visible, batches, tally):
    base = slab_base()
    caps = [STEP * visible[0, 0, view].astype(jnp.float32) for view in range(VIEWS)]

    def body(index, carry):
        half, column, rows, lanes = block_of(index)
        views = [ramps(batches[2 * view + half, column], base) for view in range(VIEWS)]
        for layer in range(LAYERS + 1):
            sums, places, weights = votes(views, caps, float(layer))
            for slot, total in enumerate(sums + [places, weights]):
                tally[slot, layer, rows, lanes] = total
        return carry

    lax.fori_loop(0, 16, body, 0)


def second_votes(visible, batches, tally, after, new_tally):
    base = slab_base()
    caps = [STEP * visible[1, 0, view].astype(jnp.float32) for view in range(VIEWS)]

    def body(index, carry):
        half, column, rows, lanes = block_of(index)
        views = [ramps(batches[2 * (VIEWS + view) + half, column], base) for view in range(VIEWS)]
        for layer in range(LAYERS):
            sums, places, weights = votes(views, caps, float(layer))
            for slot, total in enumerate(sums + [places, weights]):
                new_tally[slot, layer, rows, lanes] = tally[slot, layer, rows, lanes] + total
        return carry

    lax.fori_loop(0, 16, body, 0)


def counted(values, tally, layer):
    sums = [tally[slot, layer] for slot in range(BINS - 1)]
    return proximal(values, sums, tally[BINS - 1, layer], tally[BINS, layer])


def first_update(field, values, tally, updated, extra, side):
    for layer in range(LAYERS):
        new = counted(values[layer], tally, layer)
        updated[layer] = new
        new = 2.0 * new - field[layer]
        extra[layer] = new
        side[layer : layer + 1, :] = new[0:1, :]


def past_update(below, values, dual, tally, extra):
    extra[...] = 2.0 * counted(values[...] - 0.25 * dual[0, LAYERS - 1], tally, LAYERS) - below[...]


def top_dual(extra, past, dual, ahead, top):
    last = LAYERS - 1
    slab_end = lax.axis_index("slab") == Z_LAST
    row = ahead[last:LAYERS, :]
    top[...] = dual_layer(extra[last], past[...], row, dual[0, last], dual[1, last], dual[2, last], slab_end)[0]


def last_layers(current, dual, before, tally, updated):
    for layer in range(1, LAYERS):
        updated[layer] = counted(stepped(current, dual, None, before, layer), tally, layer)


def last_layer(current, dual, above, before, tally, updated_in, updated, layer, sem):
    layer[...] = counted(stepped(current, dual, above, before, 0), tally, 0)
    move = pltpu.make_async_copy(layer, updated.at[0], sem)
    move.start()
    move.wait()


def passed_along(value, axis, steps):
    count = lax.axis_size(axis)
    first, last = (max(0, -steps), min(count, count - steps))
    return lax.ppermute(value, axis, [(source, source + steps) for source in range(first, last)])


GROUPS = [[2 * place + half for place in range(16)] for half in range(2)]


def exchange(pieces):
    return lax.all_to_all(pieces, "slab", 0, 0, axis_index_groups=GROUPS)


def per_device(field, dual, depth, owner, visible):
    block = (LAYERS, ROWS, LANES)
    owner = pltpu.with_memory_space_constraint(owner, pltpu.HBM)
    visible = visible.transpose(0, 2, 1)

    pieces = depth.reshape(16, 8, 8, 128).transpose(0, 2, 1, 3)
    spread = exchange(pieces)

    first_layer, first_rows, field = call(
        staged, [(ROWS, LANES), (LAYERS, LANES), block], 1, [HBM], scratch_shapes=[pltpu.SemaphoreType.DMA((3,))]
    )(pltpu.with_memory_space_constraint(field, pltpu.HBM))
    below = passed_along(first_layer, "slab", -1)
    (kept,) = call(pick, [(8, 8, 128)], 1, [SMEM, VMEM])(owner, spread)
    first_rows, _ = lax.optimization_barrier((first_rows, spread))
    ahead = passed_along(first_rows, "tile", -1)
    across = lax.ppermute(kept, "slab", [(index, index ^ 1) for index in range(32)])
    below, _ = lax.optimization_barrier((below, kept))
    (below,) = call(relay, [(ROWS, LANES)], 2, [VMEM])(below)
    layer, rows = (ROWS, LANES), (LAYERS, LANES)
    dual, top, side = call(all_duals, [(3,) + block, layer, rows], 1, [VMEM] * 4)(field, dual, ahead, below)
    above = passed_along(top, "slab", 1)
    before = passed_along(side, "tile", 1)
    across, top, side = lax.optimization_barrier((across, top, side))
    (copies,) = call(copies_of, [pieces.shape], 1, [SMEM, VMEM, VMEM])(owner, kept, across)
    batches = exchange(copies)
    (values,) = call(first_values, [layer], 1, [VMEM] * 3)(field, dual, before)
    past_values = passed_along(values, "slab", -1)
    (values,) = call(all_values, [block], 5, [VMEM] * 4)(field, dual, above, before)

    (tally,) = call(first_votes, [(BINS + 1, LAYERS + 1) + layer], 12, [SMEM, VMEM])(visible, batches)
    current, extra, side = call(first_update, [block, block, rows], 1, [VMEM] * 3)(field, values, tally)
    ahead = passed_along(side, "tile", -1)
    past_values, _ = lax.optimization_barrier((past_values, side))
    (past,) = call(past_update, [layer], 1, [VMEM] * 4)(below, past_values, dual, tally)
    (top,) = call(top_dual, [layer], 1, [VMEM] * 4)(extra, past, dual, ahead)
    above = passed_along(top, "slab", 1)
    dual, side = call(second_duals, [(3,) + block, rows], 1, [VMEM] * 4 + [ANY])(extra, dual, ahead, past, top)
    before = passed_along(side, "tile", 1)
    (tally,) = call(second_votes, [(BINS + 1,) + block], 3, [SMEM, VMEM, VMEM, ANY])(visible, batches, tally, side)
    (rest,) = call(last_layers, [block], 1, [VMEM] * 4)(current, dual, before, tally)
    above, rest = lax.optimization_barrier((above, rest))
    (current,) = call(
        last_layer, [block], 1, [VMEM] * 5 + [ANY], out_specs=(ANY,), input_output_aliases={5: 0},
        scratch_shapes=[pltpu.VMEM((ROWS, LANES), jnp.float32), pltpu.SemaphoreType.DMA],
    )(current, dual, above, before, tally, rest)
    return (current, dual)


def solution(mesh):
    placed = (
        P("slab", "tile", None),
        P(None, "slab", "tile", None),
        P("slab", None, None, "tile", None),
        P(),
        P(None, None, "tile"),
    )
    return jax.shard_map(
        per_device,
        mesh=mesh,
        in_specs=placed,
        out_specs=(P("slab", "tile", None), P(None, "slab", "tile", None)),
        check_vma=False,
    )
```

```python
import jax
import jax.numpy as jnp
from jax import lax
from jax.experimental import pallas as pl
from jax.experimental.pallas import tpu as pltpu
from jax.sharding import PartitionSpec as P

VIEWS = 4
BINS = 8
BAND = 6
ITERS = 2

LAYERS = 8
ROWS = 16
LANES = 1024
STEP = 0.1
Z_LAST = 31
X_LAST = 15


def call(kernel, out_shapes, cost_us, in_specs, **more):
    return pl.pallas_call(
        kernel,
        out_shape=tuple(jax.ShapeDtypeStruct(shape, jnp.float32) for shape in out_shapes),
        in_specs=in_specs,
        compiler_params=pltpu.CompilerParams(vmem_limit_bytes=16 << 20),
        cost_estimate=pl.CostEstimate(flops=int(cost_us * 1.0e9), transcendentals=0, bytes_accessed=int(cost_us * 3.0e6)),
        name=kernel.__name__,
        **more,
    )


VMEM = pl.BlockSpec(memory_space=pltpu.VMEM)
SMEM = pl.BlockSpec(memory_space=pltpu.SMEM)
HBM = pl.BlockSpec(memory_space=pltpu.HBM)
ANY = pl.BlockSpec(memory_space=pl.ANY)


def row_ids():
    return lax.broadcasted_iota(jnp.int32, (ROWS, LANES), 0)


def lane_ids():
    return lax.broadcasted_iota(jnp.int32, (ROWS, LANES), 1)


def spread_row(row):
    return jnp.broadcast_to(row, (ROWS, LANES))


def ends():
    row, lane = row_ids(), lane_ids()
    return row, (row == ROWS - 1) & (lax.axis_index("tile") == X_LAST), lane == LANES - 1


def moved_sides(here, ahead_row, dual_x, dual_y):
    row, x_end, y_end = ends()
    ahead_x = jnp.where(row == ROWS - 1, spread_row(ahead_row), pltpu.roll(here, ROWS - 1, 0))
    ahead_y = pltpu.roll(here, LANES - 1, 1)
    moved_x = dual_x + 0.25 * jnp.where(x_end, 0.0, ahead_x - here)
    return moved_x, dual_y + 0.25 * jnp.where(y_end, 0.0, ahead_y - here)


def dual_layer(here, ahead_z, ahead_row, dual_z, dual_x, dual_y, z_end):
    _, x_end, y_end = ends()
    moved_z = dual_z + 0.25 * jnp.where(z_end, 0.0, ahead_z - here)
    moved_x, moved_y = moved_sides(here, ahead_row, dual_x, dual_y)
    norm = moved_z * moved_z + moved_x * moved_x + moved_y * moved_y
    scale = 1.0 / jnp.sqrt(jnp.maximum(norm, 1.0))
    return (
        jnp.where(z_end, 0.0, moved_z * scale),
        jnp.where(x_end, 0.0, moved_x * scale),
        jnp.where(y_end, 0.0, moved_y * scale),
    )


def pick(owner, spread, kept):
    kept[...] = spread[lax.shift_right_logical(owner[lax.shift_right_logical(lax.axis_index("slab"), 4)], 1)]


def copies_of(owner, kept, across, copies):
    slab = lax.axis_index("slab")
    here = (owner[lax.shift_right_logical(slab, 4)] & 1) == (slab & 1)
    piece = jnp.where(here, kept[...], across[...])
    for place in range(16):
        copies[place] = piece


def staged(field, first_layer, first_rows, field_here, sems):
    moves = [
        pltpu.make_async_copy(field.at[:, 0], first_rows, sems.at[0]),
        pltpu.make_async_copy(field.at[0], first_layer, sems.at[1]),
        pltpu.make_async_copy(field, field_here, sems.at[2]),
    ]
    for move in moves:
        move.start()
    for move in moves:
        move.wait()


def relay(given, same):
    same[...] = given[...]


def all_duals(field, dual, ahead, past, new_dual, top, side):
    slab_end = lax.axis_index("slab") == Z_LAST
    for layer in range(LAYERS):
        last = layer == LAYERS - 1
        dual_z, dual_x, dual_y = dual_layer(
            field[layer],
            past[...] if last else field[layer + 1],
            ahead[layer : layer + 1, :],
            dual[0, layer],
            dual[1, layer],
            dual[2, layer],
            slab_end if last else False,
        )
        new_dual[0, layer] = dual_z
        new_dual[1, layer] = dual_x
        new_dual[2, layer] = dual_y
        side[layer : layer + 1, :] = dual_x[15:16, :]
        if last:
            top[...] = dual_z


def second_duals(low, high, dual, ahead, past, after, new_dual, side):
    slab_end = lax.axis_index("slab") == Z_LAST
    for layer in range(LAYERS):
        last = layer == LAYERS - 1
        dual_z, dual_x, dual_y = dual_layer(
            joined(low, high, layer),
            past[...] if last else joined(low, high, layer + 1),
            ahead[layer : layer + 1, :],
            dual[0, layer],
            dual[1, layer],
            dual[2, layer],
            slab_end if last else False,
        )
        new_dual[0, layer] = dual_z
        new_dual[1, layer] = dual_x
        new_dual[2, layer] = dual_y
        side[layer : layer + 1, :] = dual_x[15:16, :]


def flux_of(dual, before, layer):
    row, dual_x, dual_y = spread_row(before[layer : layer + 1, :]), dual[1, layer], dual[2, layer]
    shifted = jnp.where(row_ids() == 0, row, pltpu.roll(dual_x, 1, 0))
    return (dual_x - shifted) + (dual_y - pltpu.roll(dual_y, 1, 1))


def stepped(here, dual, above, before, layer):
    prev = above[...] if layer == 0 else dual[0, layer - 1]
    return here + 0.25 * ((dual[0, layer] - prev) + flux_of(dual, before, layer))


def first_values(field, dual, before, values):
    values[...] = field[0] + 0.25 * (dual[0, 0] + flux_of(dual, before, 0))


def all_values(field, dual, above, before, values):
    for layer in range(LAYERS):
        values[layer] = stepped(field[layer], dual, above, before, layer)


def ramps(depth, base):
    away = depth - base
    return away * (0.5 * STEP * (BINS - 1) / BAND) + 0.5 * STEP * (BINS - 1), away * (STEP / BAND) + 2.0 * STEP


def votes(views, caps, layer):
    sums, places, weights = None, None, None
    for (place, weight), cap in zip(views, caps):
        q = jnp.clip(place - layer * (0.5 * STEP * (BINS - 1) / BAND), 0.0, STEP * (BINS - 1))
        w = jnp.minimum(jnp.maximum(weight - layer * (STEP / BAND), 0.0), cap)
        e = q + w
        parts = [jnp.maximum(q, jnp.minimum(e, STEP * index)) for index in range(1, BINS)]
        sums = parts if sums is None else [total + part for total, part in zip(sums, parts)]
        places = q if places is None else places + q
        weights = w if weights is None else weights + w
    return sums, places, weights


def proximal(values, sums, places, weights):
    high = values + 0.5 * weights
    best = jnp.maximum(jnp.minimum(high, -1.0), values - 0.5 * weights)
    high = high + places
    for index in range(1, BINS):
        best = jnp.maximum(best, jnp.minimum(high - sums[index - 1], -1.0 + 2.0 * index / (BINS - 1)))
    return best


def block_of(index):
    half, column = index // 8, index % 8
    return half, column, pl.ds(pl.multiple_of(half * 8, 8), 8), pl.ds(pl.multiple_of(column * 128, 128), 128)


def slab_base():
    return (lax.axis_index("slab") * LAYERS).astype(jnp.float32)


def half_votes(half, visible, batches, tally):
    base = slab_base()
    caps = [STEP * visible[0, 0, view].astype(jnp.float32) for view in range(VIEWS)]

    def body(column, carry):
        lanes = pl.ds(pl.multiple_of(column * 128, 128), 128)
        views = [ramps(batches[2 * view + half, column], base) for view in range(VIEWS)]
        for layer in range(LAYERS + 1):
            sums, places, weights = votes(views, caps, float(layer))
            for slot, total in enumerate(sums + [places, weights]):
                tally[slot, layer, :, lanes] = total
        return carry

    lax.fori_loop(0, 8, body, 0)


def low_votes(visible, batches, tally):
    half_votes(0, visible, batches, tally)


def high_votes(visible, batches, after, tally):
    half_votes(1, visible, batches, tally)


def joined(low, high, layer):
    return jnp.concatenate([low[layer], high[layer]], 0)


def second_votes(visible, batches, low, high, after, new_tally):
    base = slab_base()
    caps = [STEP * visible[1, 0, view].astype(jnp.float32) for view in range(VIEWS)]
    for half, tally in ((0, low), (1, high)):

        def body(column, carry, half=half, tally=tally):
            lanes = pl.ds(pl.multiple_of(column * 128, 128), 128)
            views = [ramps(batches[2 * (VIEWS + view) + half, column], base) for view in range(VIEWS)]
            for layer in range(LAYERS):
                sums, places, weights = votes(views, caps, float(layer))
                for slot, total in enumerate(sums + [places, weights]):
                    new_tally[slot, layer, half * 8 : half * 8 + 8, lanes] = tally[slot, layer, :, lanes] + total
            return carry

        lax.fori_loop(0, 8, body, 0)


def counted(values, tally, layer):
    sums = [tally[slot, layer] for slot in range(BINS - 1)]
    return proximal(values, sums, tally[BINS - 1, layer], tally[BINS, layer])


def low_update(field, values, tally, updated, extra, side):
    for layer in range(LAYERS):
        new = counted(values[layer, 0:8, :], tally, layer)
        updated[layer] = new
        new = 2.0 * new - field[layer, 0:8, :]
        extra[layer] = new
        side[layer : layer + 1, :] = new[0:1, :]


def high_update(field, values, tally, updated, extra):
    for layer in range(LAYERS):
        new = counted(values[layer, 8:16, :], tally, layer)
        updated[layer] = new
        extra[layer] = 2.0 * new - field[layer, 8:16, :]


def past_update(below, values, dual, low, high, extra):
    for half, tally in ((0, low), (1, high)):
        rows = slice(half * 8, half * 8 + 8)
        steps = values[rows, :] - 0.25 * dual[0, LAYERS - 1, rows, :]
        extra[rows, :] = 2.0 * counted(steps, tally, LAYERS) - below[rows, :]


def top_dual(low, high, past, dual, ahead, top):
    last = LAYERS - 1
    slab_end = lax.axis_index("slab") == Z_LAST
    here, row = joined(low, high, last), ahead[last:LAYERS, :]
    top[...] = dual_layer(here, past[...], row, dual[0, last], dual[1, last], dual[2, last], slab_end)[0]


def last_layers(low, high, dual, before, tally, updated):
    for layer in range(1, LAYERS):
        updated[layer] = counted(stepped(joined(low, high, layer), dual, None, before, layer), tally, layer)


def last_layer(low, high, dual, above, before, tally, updated_in, updated, layer, sem):
    layer[...] = counted(stepped(joined(low, high, 0), dual, above, before, 0), tally, 0)
    move = pltpu.make_async_copy(layer, updated.at[0], sem)
    move.start()
    move.wait()


def passed_along(value, axis, steps):
    count = lax.axis_size(axis)
    first, last = (max(0, -steps), min(count, count - steps))
    return lax.ppermute(value, axis, [(source, source + steps) for source in range(first, last)])


GROUPS = [[2 * place + half for place in range(16)] for half in range(2)]


def exchange(pieces):
    return lax.all_to_all(pieces, "slab", 0, 0, axis_index_groups=GROUPS)


def per_device(field, dual, depth, owner, visible):
    block = (LAYERS, ROWS, LANES)
    owner = pltpu.with_memory_space_constraint(owner, pltpu.HBM)
    visible = visible.transpose(0, 2, 1)

    pieces = depth.reshape(16, 8, 8, 128).transpose(0, 2, 1, 3)
    spread = exchange(pieces)

    first_layer, first_rows, field = call(
        staged, [(ROWS, LANES), (LAYERS, LANES), block], 1, [HBM], scratch_shapes=[pltpu.SemaphoreType.DMA((3,))]
    )(pltpu.with_memory_space_constraint(field, pltpu.HBM))
    below = passed_along(first_layer, "slab", -1)
    (kept,) = call(pick, [(8, 8, 128)], 1, [SMEM, VMEM])(owner, spread)
    first_rows, _ = lax.optimization_barrier((first_rows, spread))
    ahead = passed_along(first_rows, "tile", -1)
    across = lax.ppermute(kept, "slab", [(index, index ^ 1) for index in range(32)])
    below, _ = lax.optimization_barrier((below, kept))
    (below,) = call(relay, [(ROWS, LANES)], 2, [VMEM])(below)
    layer, rows = (ROWS, LANES), (LAYERS, LANES)
    dual, top, side = call(all_duals, [(3,) + block, layer, rows], 1, [VMEM] * 4)(field, dual, ahead, below)
    above = passed_along(top, "slab", 1)
    before = passed_along(side, "tile", 1)
    across, top, side = lax.optimization_barrier((across, top, side))
    (copies,) = call(copies_of, [pieces.shape], 1, [SMEM, VMEM, VMEM])(owner, kept, across)
    batches = exchange(copies)
    (values,) = call(first_values, [layer], 1, [VMEM] * 3)(field, dual, before)
    past_values = passed_along(values, "slab", -1)
    (values,) = call(all_values, [block], 5, [VMEM] * 4)(field, dual, above, before)

    half, count = (LAYERS, 8, LANES), (BINS + 1, LAYERS + 1, 8, LANES)
    (low_tally,) = call(low_votes, [count], 12, [SMEM, VMEM])(visible, batches)
    low, low_extra, side = call(low_update, [half, half, rows], 1, [VMEM] * 3)(field, values, low_tally)
    ahead = passed_along(side, "tile", -1)
    (high_tally,) = call(high_votes, [count], 12, [SMEM, VMEM, ANY])(visible, batches, side)
    high, high_extra = call(high_update, [half, half], 1, [VMEM] * 3)(field, values, high_tally)
    past_values, _ = lax.optimization_barrier((past_values, high))
    (past,) = call(past_update, [layer], 1, [VMEM] * 5)(below, past_values, dual, low_tally, high_tally)
    (top,) = call(top_dual, [layer], 1, [VMEM] * 5)(low_extra, high_extra, past, dual, ahead)
    above = passed_along(top, "slab", 1)
    dual, side = call(second_duals, [(3,) + block, rows], 1, [VMEM] * 5 + [ANY])(
        low_extra, high_extra, dual, ahead, past, top
    )
    before = passed_along(side, "tile", 1)
    (tally,) = call(second_votes, [(BINS + 1,) + block], 3, [SMEM] + [VMEM] * 3 + [ANY])(
        visible, batches, low_tally, high_tally, side
    )
    (rest,) = call(last_layers, [block], 1, [VMEM] * 5)(low, high, dual, before, tally)
    above, rest = lax.optimization_barrier((above, rest))
    (current,) = call(
        last_layer, [block], 1, [VMEM] * 6 + [ANY], out_specs=(ANY,), input_output_aliases={6: 0},
        scratch_shapes=[pltpu.VMEM((ROWS, LANES), jnp.float32), pltpu.SemaphoreType.DMA],
    )(low, high, dual, above, before, tally, rest)
    return (current, dual)


def solution(mesh):
    placed = (
        P("slab", "tile", None),
        P(None, "slab", "tile", None),
        P("slab", None, None, "tile", None),
        P(),
        P(None, None, "tile"),
    )
    return jax.shard_map(
        per_device,
        mesh=mesh,
        in_specs=placed,
        out_specs=(P("slab", "tile", None), P(None, "slab", "tile", None)),
        check_vma=False,
    )
```

```python
import jax
import jax.numpy as jnp
from jax import lax
from jax.experimental import pallas as pl
from jax.experimental.pallas import tpu as pltpu
from jax.sharding import PartitionSpec as P

VIEWS = 4
BINS = 8
BAND = 6
ITERS = 2

LAYERS = 8
ROWS = 16
LANES = 1024
STEP = 0.1
Z_LAST = 31
X_LAST = 15


def call(kernel, out_shapes, cost_us, in_specs, **more):
    return pl.pallas_call(
        kernel,
        out_shape=tuple(jax.ShapeDtypeStruct(shape, jnp.float32) for shape in out_shapes),
        in_specs=in_specs,
        compiler_params=pltpu.CompilerParams(vmem_limit_bytes=16 << 20),
        cost_estimate=pl.CostEstimate(flops=int(cost_us * 1.0e9), transcendentals=0, bytes_accessed=int(cost_us * 3.0e6)),
        name=kernel.__name__,
        **more,
    )


VMEM = pl.BlockSpec(memory_space=pltpu.VMEM)
SMEM = pl.BlockSpec(memory_space=pltpu.SMEM)
HBM = pl.BlockSpec(memory_space=pltpu.HBM)
ANY = pl.BlockSpec(memory_space=pl.ANY)


def row_ids():
    return lax.broadcasted_iota(jnp.int32, (ROWS, LANES), 0)


def lane_ids():
    return lax.broadcasted_iota(jnp.int32, (ROWS, LANES), 1)


def spread_row(row):
    return jnp.broadcast_to(row, (ROWS, LANES))


def ends():
    row, lane = row_ids(), lane_ids()
    return row, (row == ROWS - 1) & (lax.axis_index("tile") == X_LAST), lane == LANES - 1


def moved_sides(here, ahead_row, dual_x, dual_y):
    row, x_end, y_end = ends()
    ahead_x = jnp.where(row == ROWS - 1, spread_row(ahead_row), pltpu.roll(here, ROWS - 1, 0))
    ahead_y = pltpu.roll(here, LANES - 1, 1)
    moved_x = dual_x + 0.25 * jnp.where(x_end, 0.0, ahead_x - here)
    return moved_x, dual_y + 0.25 * jnp.where(y_end, 0.0, ahead_y - here)


def dual_layer(here, ahead_z, ahead_row, dual_z, dual_x, dual_y, z_end):
    _, x_end, y_end = ends()
    moved_z = dual_z + 0.25 * jnp.where(z_end, 0.0, ahead_z - here)
    moved_x, moved_y = moved_sides(here, ahead_row, dual_x, dual_y)
    norm = moved_z * moved_z + moved_x * moved_x + moved_y * moved_y
    scale = 1.0 / jnp.sqrt(jnp.maximum(norm, 1.0))
    return (
        jnp.where(z_end, 0.0, moved_z * scale),
        jnp.where(x_end, 0.0, moved_x * scale),
        jnp.where(y_end, 0.0, moved_y * scale),
    )


def pick(owner, spread, kept):
    kept[...] = spread[lax.shift_right_logical(owner[lax.shift_right_logical(lax.axis_index("slab"), 4)], 1)]


def copies_of(mine, kept, across, copies):
    piece = jnp.where(mine[...] > 0.5, kept[...], across[...])
    for place in range(16):
        copies[place] = piece


def staged(owner, visible, field, first_layer, first_rows, field_here, caps, mine, sems):
    moves = [
        pltpu.make_async_copy(field.at[:, 0], first_rows, sems.at[0]),
        pltpu.make_async_copy(field.at[0], first_layer, sems.at[1]),
        pltpu.make_async_copy(field, field_here, sems.at[2]),
    ]
    for move in moves:
        move.start()
    for view in range(ITERS * VIEWS):
        cap = STEP * visible[view // VIEWS, 0, view % VIEWS].astype(jnp.float32)
        caps[view] = jnp.full((8, 128), cap, jnp.float32)
    slab = lax.axis_index("slab")
    here = (owner[lax.shift_right_logical(slab, 4)] & 1) == (slab & 1)
    mine[...] = jnp.full((8, 128), jnp.where(here, 1.0, 0.0), jnp.float32)
    for move in moves:
        move.wait()


def relay(given, same):
    same[...] = given[...]


def all_duals(field, dual, ahead, past, new_dual, top, side):
    slab_end = lax.axis_index("slab") == Z_LAST
    for layer in range(LAYERS):
        last = layer == LAYERS - 1
        dual_z, dual_x, dual_y = dual_layer(
            field[layer],
            past[...] if last else field[layer + 1],
            ahead[layer : layer + 1, :],
            dual[0, layer],
            dual[1, layer],
            dual[2, layer],
            slab_end if last else False,
        )
        new_dual[0, layer] = dual_z
        new_dual[1, layer] = dual_x
        new_dual[2, layer] = dual_y
        side[layer : layer + 1, :] = dual_x[15:16, :]
        if last:
            top[...] = dual_z


def second_duals(low, high, dual, ahead, past, after, new_dual, side):
    slab_end = lax.axis_index("slab") == Z_LAST
    for layer in range(LAYERS):
        last = layer == LAYERS - 1
        dual_z, dual_x, dual_y = dual_layer(
            joined(low, high, layer),
            past[...] if last else joined(low, high, layer + 1),
            ahead[layer : layer + 1, :],
            dual[0, layer],
            dual[1, layer],
            dual[2, layer],
            slab_end if last else False,
        )
        new_dual[0, layer] = dual_z
        new_dual[1, layer] = dual_x
        new_dual[2, layer] = dual_y
        side[layer : layer + 1, :] = dual_x[15:16, :]


def flux_of(dual, before, layer):
    row, dual_x, dual_y = spread_row(before[layer : layer + 1, :]), dual[1, layer], dual[2, layer]
    shifted = jnp.where(row_ids() == 0, row, pltpu.roll(dual_x, 1, 0))
    return (dual_x - shifted) + (dual_y - pltpu.roll(dual_y, 1, 1))


def stepped(here, dual, above, before, layer):
    prev = above[...] if layer == 0 else dual[0, layer - 1]
    return here + 0.25 * ((dual[0, layer] - prev) + flux_of(dual, before, layer))


def first_values(field, dual, before, values):
    values[...] = field[0] + 0.25 * (dual[0, 0] + flux_of(dual, before, 0))


def all_values(field, dual, above, before, values):
    for layer in range(LAYERS):
        values[layer] = stepped(field[layer], dual, above, before, layer)


def ramps(depth, base):
    away = depth - base
    return away * (0.5 * STEP * (BINS - 1) / BAND) + 0.5 * STEP * (BINS - 1), away * (STEP / BAND) + 2.0 * STEP


def votes(views, caps, layer):
    sums, places, weights = None, None, None
    for (place, weight), cap in zip(views, caps):
        q = jnp.clip(place - layer * (0.5 * STEP * (BINS - 1) / BAND), 0.0, STEP * (BINS - 1))
        w = jnp.minimum(jnp.maximum(weight - layer * (STEP / BAND), 0.0), cap)
        e = q + w
        parts = [jnp.maximum(q, jnp.minimum(e, STEP * index)) for index in range(1, BINS)]
        sums = parts if sums is None else [total + part for total, part in zip(sums, parts)]
        places = q if places is None else places + q
        weights = w if weights is None else weights + w
    return sums, places, weights


def proximal(values, sums, places, weights):
    high = values + 0.5 * weights
    best = jnp.maximum(jnp.minimum(high, -1.0), values - 0.5 * weights)
    high = high + places
    for index in range(1, BINS):
        best = jnp.maximum(best, jnp.minimum(high - sums[index - 1], -1.0 + 2.0 * index / (BINS - 1)))
    return best


def block_of(index):
    half, column = index // 8, index % 8
    return half, column, pl.ds(pl.multiple_of(half * 8, 8), 8), pl.ds(pl.multiple_of(column * 128, 128), 128)


def slab_base():
    return (lax.axis_index("slab") * LAYERS).astype(jnp.float32)


def half_votes(half, caps_of, batches, tally):
    base = slab_base()
    caps = [caps_of[view] for view in range(VIEWS)]

    def body(column, carry):
        lanes = pl.ds(pl.multiple_of(column * 128, 128), 128)
        views = [ramps(batches[2 * view + half, column], base) for view in range(VIEWS)]
        for layer in range(LAYERS + 1):
            sums, places, weights = votes(views, caps, float(layer))
            for slot, total in enumerate(sums + [places, weights]):
                tally[slot, layer, :, lanes] = total
        return carry

    lax.fori_loop(0, 8, body, 0)


def low_votes(caps, batches, tally):
    half_votes(0, caps, batches, tally)


def high_votes(caps, batches, after, tally):
    half_votes(1, caps, batches, tally)


def joined(low, high, layer):
    return jnp.concatenate([low[layer], high[layer]], 0)


def second_votes(caps_of, batches, low, high, after, new_tally):
    base = slab_base()
    caps = [caps_of[VIEWS + view] for view in range(VIEWS)]
    for half, tally in ((0, low), (1, high)):

        def body(column, carry, half=half, tally=tally):
            lanes = pl.ds(pl.multiple_of(column * 128, 128), 128)
            views = [ramps(batches[2 * (VIEWS + view) + half, column], base) for view in range(VIEWS)]
            for layer in range(LAYERS):
                sums, places, weights = votes(views, caps, float(layer))
                for slot, total in enumerate(sums + [places, weights]):
                    new_tally[slot, layer, half * 8 : half * 8 + 8, lanes] = tally[slot, layer, :, lanes] + total
            return carry

        lax.fori_loop(0, 8, body, 0)


def counted(values, tally, layer):
    sums = [tally[slot, layer] for slot in range(BINS - 1)]
    return proximal(values, sums, tally[BINS - 1, layer], tally[BINS, layer])


def low_update(field, values, tally, updated, extra, side):
    for layer in range(LAYERS):
        new = counted(values[layer, 0:8, :], tally, layer)
        updated[layer] = new
        new = 2.0 * new - field[layer, 0:8, :]
        extra[layer] = new
        side[layer : layer + 1, :] = new[0:1, :]


def high_update(field, values, tally, updated, extra):
    for layer in range(LAYERS):
        new = counted(values[layer, 8:16, :], tally, layer)
        updated[layer] = new
        extra[layer] = 2.0 * new - field[layer, 8:16, :]


def past_update(below, values, dual, low, high, extra):
    for half, tally in ((0, low), (1, high)):
        rows = slice(half * 8, half * 8 + 8)
        steps = values[rows, :] - 0.25 * dual[0, LAYERS - 1, rows, :]
        extra[rows, :] = 2.0 * counted(steps, tally, LAYERS) - below[rows, :]


def top_dual(low, high, past, dual, ahead, top):
    last = LAYERS - 1
    slab_end = lax.axis_index("slab") == Z_LAST
    here, row = joined(low, high, last), ahead[last:LAYERS, :]
    top[...] = dual_layer(here, past[...], row, dual[0, last], dual[1, last], dual[2, last], slab_end)[0]


def last_layers(low, high, dual, before, tally, updated):
    for layer in range(1, LAYERS):
        updated[layer] = counted(stepped(joined(low, high, layer), dual, None, before, layer), tally, layer)


def last_layer(low, high, dual, above, before, tally, updated_in, updated, layer, sem):
    layer[...] = counted(stepped(joined(low, high, 0), dual, above, before, 0), tally, 0)
    move = pltpu.make_async_copy(layer, updated.at[0], sem)
    move.start()
    move.wait()


def passed_along(value, axis, steps):
    count = lax.axis_size(axis)
    first, last = (max(0, -steps), min(count, count - steps))
    return lax.ppermute(value, axis, [(source, source + steps) for source in range(first, last)])


GROUPS = [[2 * place + half for place in range(16)] for half in range(2)]


def exchange(pieces):
    return lax.all_to_all(pieces, "slab", 0, 0, axis_index_groups=GROUPS)


def per_device(field, dual, depth, owner, visible):
    block = (LAYERS, ROWS, LANES)
    owner = pltpu.with_memory_space_constraint(owner, pltpu.HBM)
    visible = pltpu.with_memory_space_constraint(visible.transpose(0, 2, 1), pltpu.HBM)

    pieces = depth.reshape(16, 8, 8, 128).transpose(0, 2, 1, 3)
    spread = exchange(pieces)

    first_layer, first_rows, field, caps, mine = call(
        staged, [(ROWS, LANES), (LAYERS, LANES), block, (ITERS * VIEWS, 8, 128), (8, 128)], 1, [SMEM, SMEM, HBM],
        scratch_shapes=[pltpu.SemaphoreType.DMA((3,))],
    )(owner, visible, pltpu.with_memory_space_constraint(field, pltpu.HBM))
    below = passed_along(first_layer, "slab", -1)
    (kept,) = call(pick, [(8, 8, 128)], 1, [SMEM, VMEM])(owner, spread)
    first_rows, _ = lax.optimization_barrier((first_rows, spread))
    ahead = passed_along(first_rows, "tile", -1)
    across = lax.ppermute(kept, "slab", [(index, index ^ 1) for index in range(32)])
    below, _ = lax.optimization_barrier((below, kept))
    (below,) = call(relay, [(ROWS, LANES)], 2, [VMEM])(below)
    layer, rows = (ROWS, LANES), (LAYERS, LANES)
    dual, top, side = call(all_duals, [(3,) + block, layer, rows], 1, [VMEM] * 4)(field, dual, ahead, below)
    above = passed_along(top, "slab", 1)
    before = passed_along(side, "tile", 1)
    across, top, side = lax.optimization_barrier((across, top, side))
    (copies,) = call(copies_of, [pieces.shape], 1, [VMEM] * 3)(mine, kept, across)
    batches = exchange(copies)
    (values,) = call(first_values, [layer], 1, [VMEM] * 3)(field, dual, before)
    past_values = passed_along(values, "slab", -1)
    (values,) = call(all_values, [block], 5, [VMEM] * 4)(field, dual, above, before)

    half, count = (LAYERS, 8, LANES), (BINS + 1, LAYERS + 1, 8, LANES)
    (low_tally,) = call(low_votes, [count], 12, [VMEM, VMEM])(caps, batches)
    low, low_extra, side = call(low_update, [half, half, rows], 1, [VMEM] * 3)(field, values, low_tally)
    ahead = passed_along(side, "tile", -1)
    (high_tally,) = call(high_votes, [count], 12, [VMEM, VMEM, ANY])(caps, batches, side)
    high, high_extra = call(high_update, [half, half], 1, [VMEM] * 3)(field, values, high_tally)
    past_values, _ = lax.optimization_barrier((past_values, high))
    (past,) = call(past_update, [layer], 1, [VMEM] * 5)(below, past_values, dual, low_tally, high_tally)
    (top,) = call(top_dual, [layer], 1, [VMEM] * 5)(low_extra, high_extra, past, dual, ahead)
    above = passed_along(top, "slab", 1)
    dual, side = call(second_duals, [(3,) + block, rows], 1, [VMEM] * 5 + [ANY])(
        low_extra, high_extra, dual, ahead, past, top
    )
    before = passed_along(side, "tile", 1)
    (tally,) = call(second_votes, [(BINS + 1,) + block], 3, [VMEM] * 4 + [ANY])(
        caps, batches, low_tally, high_tally, side
    )
    (rest,) = call(last_layers, [block], 1, [VMEM] * 5)(low, high, dual, before, tally)
    above, rest = lax.optimization_barrier((above, rest))
    (current,) = call(
        last_layer, [block], 1, [VMEM] * 6 + [ANY], out_specs=(ANY,), input_output_aliases={6: 0},
        scratch_shapes=[pltpu.VMEM((ROWS, LANES), jnp.float32), pltpu.SemaphoreType.DMA],
    )(low, high, dual, above, before, tally, rest)
    return (current, dual)


def solution(mesh):
    placed = (
        P("slab", "tile", None),
        P(None, "slab", "tile", None),
        P("slab", None, None, "tile", None),
        P(),
        P(None, None, "tile"),
    )
    return jax.shard_map(
        per_device,
        mesh=mesh,
        in_specs=placed,
        out_specs=(P("slab", "tile", None), P(None, "slab", "tile", None)),
        check_vma=False,
    )
```

```python
import jax
import jax.numpy as jnp
from jax import lax
from jax.experimental import pallas as pl
from jax.experimental.pallas import tpu as pltpu
from jax.sharding import PartitionSpec as P

VIEWS = 4
BINS = 8
BAND = 6
ITERS = 2

LAYERS = 8
ROWS = 16
LANES = 1024
STEP = 0.1
Z_LAST = 31
X_LAST = 15


def call(kernel, out_shapes, cost_us, in_specs, **more):
    return pl.pallas_call(
        kernel,
        out_shape=tuple(jax.ShapeDtypeStruct(shape, jnp.float32) for shape in out_shapes),
        in_specs=in_specs,
        compiler_params=pltpu.CompilerParams(vmem_limit_bytes=16 << 20),
        cost_estimate=pl.CostEstimate(flops=int(cost_us * 1.0e9), transcendentals=0, bytes_accessed=int(cost_us * 3.0e6)),
        name=kernel.__name__,
        **more,
    )


VMEM = pl.BlockSpec(memory_space=pltpu.VMEM)
SMEM = pl.BlockSpec(memory_space=pltpu.SMEM)
HBM = pl.BlockSpec(memory_space=pltpu.HBM)
ANY = pl.BlockSpec(memory_space=pl.ANY)


def row_ids():
    return lax.broadcasted_iota(jnp.int32, (ROWS, LANES), 0)


def lane_ids():
    return lax.broadcasted_iota(jnp.int32, (ROWS, LANES), 1)


def spread_row(row):
    return jnp.broadcast_to(row, (ROWS, LANES))


def ends():
    row, lane = row_ids(), lane_ids()
    return row, (row == ROWS - 1) & (lax.axis_index("tile") == X_LAST), lane == LANES - 1


def moved_sides(here, ahead_row, dual_x, dual_y):
    row, x_end, y_end = ends()
    ahead_x = jnp.where(row == ROWS - 1, spread_row(ahead_row), pltpu.roll(here, ROWS - 1, 0))
    ahead_y = pltpu.roll(here, LANES - 1, 1)
    moved_x = dual_x + 0.25 * jnp.where(x_end, 0.0, ahead_x - here)
    return moved_x, dual_y + 0.25 * jnp.where(y_end, 0.0, ahead_y - here)


def dual_layer(here, ahead_z, ahead_row, dual_z, dual_x, dual_y, z_end):
    _, x_end, y_end = ends()
    moved_z = dual_z + 0.25 * jnp.where(z_end, 0.0, ahead_z - here)
    moved_x, moved_y = moved_sides(here, ahead_row, dual_x, dual_y)
    norm = moved_z * moved_z + moved_x * moved_x + moved_y * moved_y
    scale = 1.0 / jnp.sqrt(jnp.maximum(norm, 1.0))
    return (
        jnp.where(z_end, 0.0, moved_z * scale),
        jnp.where(x_end, 0.0, moved_x * scale),
        jnp.where(y_end, 0.0, moved_y * scale),
    )


def pick(owner, spread, kept):
    kept[...] = spread[lax.shift_right_logical(owner[lax.shift_right_logical(lax.axis_index("slab"), 4)], 1)]


def copies_of(mine, kept, across, copies):
    piece = jnp.where(mine[...] > 0.5, kept[...], across[...])
    for place in range(16):
        copies[place] = piece


def staged(owner_far, visible_far, field, first_layer, first_rows, field_here, caps, mine, owner, visible, sems):
    moves = [
        pltpu.make_async_copy(field.at[:, 0], first_rows, sems.at[0]),
        pltpu.make_async_copy(field.at[0], first_layer, sems.at[1]),
        pltpu.make_async_copy(field, field_here, sems.at[2]),
    ]
    scalars = [
        pltpu.make_async_copy(owner_far, owner, sems.at[3]),
        pltpu.make_async_copy(visible_far, visible, sems.at[4]),
    ]
    for scalar in scalars:
        scalar.start()
    for move in moves:
        move.start()
    for scalar in scalars:
        scalar.wait()
    for view in range(ITERS * VIEWS):
        cap = STEP * visible[view // VIEWS, 0, view % VIEWS].astype(jnp.float32)
        caps[view] = jnp.full((8, 128), cap, jnp.float32)
    slab = lax.axis_index("slab")
    here = (owner[lax.shift_right_logical(slab, 4)] & 1) == (slab & 1)
    mine[...] = jnp.full((8, 128), jnp.where(here, 1.0, 0.0), jnp.float32)
    for move in moves:
        move.wait()


def relay(given, same):
    same[...] = given[...]


def all_duals(field, dual, ahead, past, new_dual, top, side):
    slab_end = lax.axis_index("slab") == Z_LAST
    for layer in range(LAYERS):
        last = layer == LAYERS - 1
        dual_z, dual_x, dual_y = dual_layer(
            field[layer],
            past[...] if last else field[layer + 1],
            ahead[layer : layer + 1, :],
            dual[0, layer],
            dual[1, layer],
            dual[2, layer],
            slab_end if last else False,
        )
        new_dual[0, layer] = dual_z
        new_dual[1, layer] = dual_x
        new_dual[2, layer] = dual_y
        side[layer : layer + 1, :] = dual_x[15:16, :]
        if last:
            top[...] = dual_z


def second_duals(low, high, dual, ahead, past, after, new_dual, side):
    slab_end = lax.axis_index("slab") == Z_LAST
    for layer in range(LAYERS):
        last = layer == LAYERS - 1
        dual_z, dual_x, dual_y = dual_layer(
            joined(low, high, layer),
            past[...] if last else joined(low, high, layer + 1),
            ahead[layer : layer + 1, :],
            dual[0, layer],
            dual[1, layer],
            dual[2, layer],
            slab_end if last else False,
        )
        new_dual[0, layer] = dual_z
        new_dual[1, layer] = dual_x
        new_dual[2, layer] = dual_y
        side[layer : layer + 1, :] = dual_x[15:16, :]


def flux_of(dual, before, layer):
    row, dual_x, dual_y = spread_row(before[layer : layer + 1, :]), dual[1, layer], dual[2, layer]
    shifted = jnp.where(row_ids() == 0, row, pltpu.roll(dual_x, 1, 0))
    return (dual_x - shifted) + (dual_y - pltpu.roll(dual_y, 1, 1))


def stepped(here, dual, above, before, layer):
    prev = above[...] if layer == 0 else dual[0, layer - 1]
    return here + 0.25 * ((dual[0, layer] - prev) + flux_of(dual, before, layer))


def first_values(field, dual, before, values):
    values[...] = field[0] + 0.25 * (dual[0, 0] + flux_of(dual, before, 0))


def all_values(field, dual, above, before, values):
    for layer in range(LAYERS):
        values[layer] = stepped(field[layer], dual, above, before, layer)


def ramps(depth, base):
    away = depth - base
    return away * (0.5 * STEP * (BINS - 1) / BAND) + 0.5 * STEP * (BINS - 1), away * (STEP / BAND) + 2.0 * STEP


def votes(views, caps, layer):
    sums, places, weights = None, None, None
    for (place, weight), cap in zip(views, caps):
        q = jnp.clip(place - layer * (0.5 * STEP * (BINS - 1) / BAND), 0.0, STEP * (BINS - 1))
        w = jnp.minimum(jnp.maximum(weight - layer * (STEP / BAND), 0.0), cap)
        e = q + w
        parts = [jnp.maximum(q, jnp.minimum(e, STEP * index)) for index in range(1, BINS)]
        sums = parts if sums is None else [total + part for total, part in zip(sums, parts)]
        places = q if places is None else places + q
        weights = w if weights is None else weights + w
    return sums, places, weights


def proximal(values, sums, places, weights):
    high = values + 0.5 * weights
    best = jnp.maximum(jnp.minimum(high, -1.0), values - 0.5 * weights)
    high = high + places
    for index in range(1, BINS):
        best = jnp.maximum(best, jnp.minimum(high - sums[index - 1], -1.0 + 2.0 * index / (BINS - 1)))
    return best


def block_of(index):
    half, column = index // 8, index % 8
    return half, column, pl.ds(pl.multiple_of(half * 8, 8), 8), pl.ds(pl.multiple_of(column * 128, 128), 128)


def slab_base():
    return (lax.axis_index("slab") * LAYERS).astype(jnp.float32)


def half_votes(half, caps_of, batches, tally):
    base = slab_base()
    caps = [caps_of[view] for view in range(VIEWS)]

    def body(column, carry):
        lanes = pl.ds(pl.multiple_of(column * 128, 128), 128)
        views = [ramps(batches[2 * view + half, column], base) for view in range(VIEWS)]
        for layer in range(LAYERS + 1):
            sums, places, weights = votes(views, caps, float(layer))
            for slot, total in enumerate(sums + [places, weights]):
                tally[slot, layer, :, lanes] = total
        return carry

    lax.fori_loop(0, 8, body, 0)


def low_votes(caps, batches, tally):
    half_votes(0, caps, batches, tally)


def high_votes(caps, batches, after, tally):
    half_votes(1, caps, batches, tally)


def joined(low, high, layer):
    return jnp.concatenate([low[layer], high[layer]], 0)


def second_votes(caps_of, batches, low, high, after, new_tally):
    base = slab_base()
    caps = [caps_of[VIEWS + view] for view in range(VIEWS)]
    for half, tally in ((0, low), (1, high)):

        def body(column, carry, half=half, tally=tally):
            lanes = pl.ds(pl.multiple_of(column * 128, 128), 128)
            views = [ramps(batches[2 * (VIEWS + view) + half, column], base) for view in range(VIEWS)]
            for layer in range(LAYERS):
                sums, places, weights = votes(views, caps, float(layer))
                for slot, total in enumerate(sums + [places, weights]):
                    new_tally[slot, layer, half * 8 : half * 8 + 8, lanes] = tally[slot, layer, :, lanes] + total
            return carry

        lax.fori_loop(0, 8, body, 0)


def counted(values, tally, layer):
    sums = [tally[slot, layer] for slot in range(BINS - 1)]
    return proximal(values, sums, tally[BINS - 1, layer], tally[BINS, layer])


def low_update(field, values, tally, updated, extra, side):
    for layer in range(LAYERS):
        new = counted(values[layer, 0:8, :], tally, layer)
        updated[layer] = new
        new = 2.0 * new - field[layer, 0:8, :]
        extra[layer] = new
        side[layer : layer + 1, :] = new[0:1, :]


def high_update(field, values, tally, updated, extra):
    for layer in range(LAYERS):
        new = counted(values[layer, 8:16, :], tally, layer)
        updated[layer] = new
        extra[layer] = 2.0 * new - field[layer, 8:16, :]


def past_update(below, values, dual, low, high, extra):
    for half, tally in ((0, low), (1, high)):
        rows = slice(half * 8, half * 8 + 8)
        steps = values[rows, :] - 0.25 * dual[0, LAYERS - 1, rows, :]
        extra[rows, :] = 2.0 * counted(steps, tally, LAYERS) - below[rows, :]


def top_dual(low, high, past, dual, ahead, top):
    last = LAYERS - 1
    slab_end = lax.axis_index("slab") == Z_LAST
    here, row = joined(low, high, last), ahead[last:LAYERS, :]
    top[...] = dual_layer(here, past[...], row, dual[0, last], dual[1, last], dual[2, last], slab_end)[0]


def last_layers(low, high, dual, before, tally, updated):
    for layer in range(1, LAYERS):
        updated[layer] = counted(stepped(joined(low, high, layer), dual, None, before, layer), tally, layer)


def last_layer(low, high, dual, above, before, tally, updated_in, updated, layer, sem):
    layer[...] = counted(stepped(joined(low, high, 0), dual, above, before, 0), tally, 0)
    move = pltpu.make_async_copy(layer, updated.at[0], sem)
    move.start()
    move.wait()


def passed_along(value, axis, steps):
    count = lax.axis_size(axis)
    first, last = (max(0, -steps), min(count, count - steps))
    return lax.ppermute(value, axis, [(source, source + steps) for source in range(first, last)])


GROUPS = [[2 * place + half for place in range(16)] for half in range(2)]


def exchange(pieces):
    return lax.all_to_all(pieces, "slab", 0, 0, axis_index_groups=GROUPS)


def per_device(field, dual, depth, owner, visible):
    block = (LAYERS, ROWS, LANES)
    owner = pltpu.with_memory_space_constraint(owner, pltpu.HBM)
    visible = pltpu.with_memory_space_constraint(visible.transpose(0, 2, 1), pltpu.HBM)

    pieces = depth.reshape(16, 8, 8, 128).transpose(0, 2, 1, 3)
    spread = exchange(pieces)

    first_layer, first_rows, field, caps, mine = call(
        staged, [(ROWS, LANES), (LAYERS, LANES), block, (ITERS * VIEWS, 8, 128), (8, 128)], 1, [HBM] * 3,
        scratch_shapes=[
            pltpu.SMEM((ITERS,), jnp.int32), pltpu.SMEM((ITERS, 1, VIEWS), jnp.int32), pltpu.SemaphoreType.DMA((5,))
        ],
    )(owner, visible, pltpu.with_memory_space_constraint(field, pltpu.HBM))
    below = passed_along(first_layer, "slab", -1)
    (kept,) = call(pick, [(8, 8, 128)], 1, [SMEM, VMEM])(owner, spread)
    first_rows, _ = lax.optimization_barrier((first_rows, spread))
    ahead = passed_along(first_rows, "tile", -1)
    across = lax.ppermute(kept, "slab", [(index, index ^ 1) for index in range(32)])
    below, _ = lax.optimization_barrier((below, kept))
    (below,) = call(relay, [(ROWS, LANES)], 2, [VMEM])(below)
    layer, rows = (ROWS, LANES), (LAYERS, LANES)
    dual, top, side = call(all_duals, [(3,) + block, layer, rows], 1, [VMEM] * 4)(field, dual, ahead, below)
    above = passed_along(top, "slab", 1)
    before = passed_along(side, "tile", 1)
    across, top, side = lax.optimization_barrier((across, top, side))
    (copies,) = call(copies_of, [pieces.shape], 1, [VMEM] * 3)(mine, kept, across)
    batches = exchange(copies)
    (values,) = call(first_values, [layer], 1, [VMEM] * 3)(field, dual, before)
    past_values = passed_along(values, "slab", -1)
    (values,) = call(all_values, [block], 5, [VMEM] * 4)(field, dual, above, before)

    half, count = (LAYERS, 8, LANES), (BINS + 1, LAYERS + 1, 8, LANES)
    (low_tally,) = call(low_votes, [count], 12, [VMEM, VMEM])(caps, batches)
    low, low_extra, side = call(low_update, [half, half, rows], 1, [VMEM] * 3)(field, values, low_tally)
    ahead = passed_along(side, "tile", -1)
    (high_tally,) = call(high_votes, [count], 12, [VMEM, VMEM, ANY])(caps, batches, side)
    high, high_extra = call(high_update, [half, half], 1, [VMEM] * 3)(field, values, high_tally)
    past_values, _ = lax.optimization_barrier((past_values, high))
    (past,) = call(past_update, [layer], 1, [VMEM] * 5)(below, past_values, dual, low_tally, high_tally)
    (top,) = call(top_dual, [layer], 1, [VMEM] * 5)(low_extra, high_extra, past, dual, ahead)
    above = passed_along(top, "slab", 1)
    dual, side = call(second_duals, [(3,) + block, rows], 1, [VMEM] * 5 + [ANY])(
        low_extra, high_extra, dual, ahead, past, top
    )
    before = passed_along(side, "tile", 1)
    (tally,) = call(second_votes, [(BINS + 1,) + block], 3, [VMEM] * 4 + [ANY])(
        caps, batches, low_tally, high_tally, side
    )
    (rest,) = call(last_layers, [block], 1, [VMEM] * 5)(low, high, dual, before, tally)
    above, rest = lax.optimization_barrier((above, rest))
    (current,) = call(
        last_layer, [block], 1, [VMEM] * 6 + [ANY], out_specs=(ANY,), input_output_aliases={6: 0},
        scratch_shapes=[pltpu.VMEM((ROWS, LANES), jnp.float32), pltpu.SemaphoreType.DMA],
    )(low, high, dual, above, before, tally, rest)
    return (current, dual)


def solution(mesh):
    placed = (
        P("slab", "tile", None),
        P(None, "slab", "tile", None),
        P("slab", None, None, "tile", None),
        P(),
        P(None, None, "tile"),
    )
    return jax.shard_map(
        per_device,
        mesh=mesh,
        in_specs=placed,
        out_specs=(P("slab", "tile", None), P(None, "slab", "tile", None)),
        check_vma=False,
    )
```

```python
import jax
import jax.numpy as jnp
from jax import lax
from jax.experimental import pallas as pl
from jax.experimental.pallas import tpu as pltpu
from jax.sharding import PartitionSpec as P

VIEWS = 4
BINS = 8
BAND = 6
ITERS = 2

LAYERS = 8
ROWS = 16
LANES = 1024
STEP = 0.1
Z_LAST = 31
X_LAST = 15


def call(kernel, out_shapes, cost_us, in_specs, **more):
    return pl.pallas_call(
        kernel,
        out_shape=tuple(jax.ShapeDtypeStruct(shape, jnp.float32) for shape in out_shapes),
        in_specs=in_specs,
        compiler_params=pltpu.CompilerParams(vmem_limit_bytes=16 << 20),
        cost_estimate=pl.CostEstimate(flops=int(cost_us * 1.0e9), transcendentals=0, bytes_accessed=int(cost_us * 3.0e6)),
        name=kernel.__name__,
        **more,
    )


VMEM = pl.BlockSpec(memory_space=pltpu.VMEM)
SMEM = pl.BlockSpec(memory_space=pltpu.SMEM)
HBM = pl.BlockSpec(memory_space=pltpu.HBM)
ANY = pl.BlockSpec(memory_space=pl.ANY)


def row_ids():
    return lax.broadcasted_iota(jnp.int32, (ROWS, LANES), 0)


def lane_ids():
    return lax.broadcasted_iota(jnp.int32, (ROWS, LANES), 1)


def spread_row(row):
    return jnp.broadcast_to(row, (ROWS, LANES))


def ends():
    row, lane = row_ids(), lane_ids()
    return row, (row == ROWS - 1) & (lax.axis_index("tile") == X_LAST), lane == LANES - 1


def moved_sides(here, ahead_row, dual_x, dual_y):
    row, x_end, y_end = ends()
    ahead_x = jnp.where(row == ROWS - 1, spread_row(ahead_row), pltpu.roll(here, ROWS - 1, 0))
    ahead_y = pltpu.roll(here, LANES - 1, 1)
    moved_x = dual_x + 0.25 * jnp.where(x_end, 0.0, ahead_x - here)
    return moved_x, dual_y + 0.25 * jnp.where(y_end, 0.0, ahead_y - here)


def dual_layer(here, ahead_z, ahead_row, dual_z, dual_x, dual_y, z_end):
    _, x_end, y_end = ends()
    moved_z = dual_z + 0.25 * jnp.where(z_end, 0.0, ahead_z - here)
    moved_x, moved_y = moved_sides(here, ahead_row, dual_x, dual_y)
    norm = moved_z * moved_z + moved_x * moved_x + moved_y * moved_y
    scale = 1.0 / jnp.sqrt(jnp.maximum(norm, 1.0))
    return (
        jnp.where(z_end, 0.0, moved_z * scale),
        jnp.where(x_end, 0.0, moved_x * scale),
        jnp.where(y_end, 0.0, moved_y * scale),
    )


def pick(owner, spread, kept):
    kept[...] = spread[lax.shift_right_logical(owner[lax.shift_right_logical(lax.axis_index("slab"), 4)], 1)]


def copies_of(mine, kept, across, copies):
    piece = jnp.where(mine[...] > 0.5, kept[...], across[...])
    for place in range(16):
        copies[place] = piece


def staged(owner_far, visible_far, field, first_layer, first_rows, field_here, caps, mine, owner, visible, sems):
    moves = [
        pltpu.make_async_copy(field.at[:, 0], first_rows, sems.at[0]),
        pltpu.make_async_copy(field.at[0], first_layer, sems.at[1]),
        pltpu.make_async_copy(field, field_here, sems.at[2]),
    ]
    scalars = [
        pltpu.make_async_copy(owner_far, owner, sems.at[3]),
        pltpu.make_async_copy(visible_far, visible, sems.at[4]),
    ]
    for scalar in scalars:
        scalar.start()
    for move in moves:
        move.start()
    for scalar in scalars:
        scalar.wait()
    for view in range(ITERS * VIEWS):
        cap = STEP * visible[view // VIEWS, 0, view % VIEWS].astype(jnp.float32)
        caps[view] = jnp.full((8, 128), cap, jnp.float32)
    slab = lax.axis_index("slab")
    here = (owner[lax.shift_right_logical(slab, 4)] & 1) == (slab & 1)
    mine[...] = jnp.full((8, 128), jnp.where(here, 1.0, 0.0), jnp.float32)
    for move in moves:
        move.wait()


def relay(given, same):
    same[...] = given[...]


def all_duals(field, dual, ahead, past, new_dual, top, side):
    slab_end = lax.axis_index("slab") == Z_LAST
    for layer in range(LAYERS):
        last = layer == LAYERS - 1
        dual_z, dual_x, dual_y = dual_layer(
            field[layer],
            past[...] if last else field[layer + 1],
            ahead[layer : layer + 1, :],
            dual[0, layer],
            dual[1, layer],
            dual[2, layer],
            slab_end if last else False,
        )
        new_dual[0, layer] = dual_z
        new_dual[1, layer] = dual_x
        new_dual[2, layer] = dual_y
        side[layer : layer + 1, :] = dual_x[15:16, :]
        if last:
            top[...] = dual_z


def second_duals(low, high, dual, ahead, past, after, new_dual, side):
    slab_end = lax.axis_index("slab") == Z_LAST
    for layer in range(LAYERS):
        last = layer == LAYERS - 1
        dual_z, dual_x, dual_y = dual_layer(
            joined(low, high, layer),
            past[...] if last else joined(low, high, layer + 1),
            ahead[layer : layer + 1, :],
            dual[0, layer],
            dual[1, layer],
            dual[2, layer],
            slab_end if last else False,
        )
        new_dual[0, layer] = dual_z
        new_dual[1, layer] = dual_x
        new_dual[2, layer] = dual_y
        side[layer : layer + 1, :] = dual_x[15:16, :]


def flux_of(dual, before, layer):
    row, dual_x, dual_y = spread_row(before[layer : layer + 1, :]), dual[1, layer], dual[2, layer]
    shifted = jnp.where(row_ids() == 0, row, pltpu.roll(dual_x, 1, 0))
    return (dual_x - shifted) + (dual_y - pltpu.roll(dual_y, 1, 1))


def stepped(here, dual, above, before, layer):
    prev = above[...] if layer == 0 else dual[0, layer - 1]
    return here + 0.25 * ((dual[0, layer] - prev) + flux_of(dual, before, layer))


def first_values(field, dual, before, values):
    values[...] = field[0] + 0.25 * (dual[0, 0] + flux_of(dual, before, 0))


def all_values(field, dual, above, before, values):
    for layer in range(LAYERS):
        values[layer] = stepped(field[layer], dual, above, before, layer)


def ramps(depth, base):
    away = depth - base
    return away * (0.5 * STEP * (BINS - 1) / BAND) + 0.5 * STEP * (BINS - 1), away * (STEP / BAND) + 2.0 * STEP


def votes(views, caps, layer):
    sums, places, weights = None, None, None
    for (place, weight), cap in zip(views, caps):
        q = jnp.clip(place - layer * (0.5 * STEP * (BINS - 1) / BAND), 0.0, STEP * (BINS - 1))
        w = jnp.minimum(jnp.maximum(weight - layer * (STEP / BAND), 0.0), cap)
        e = q + w
        parts = [jnp.maximum(q, jnp.minimum(e, STEP * index)) for index in range(1, BINS)]
        sums = parts if sums is None else [total + part for total, part in zip(sums, parts)]
        places = q if places is None else places + q
        weights = w if weights is None else weights + w
    return sums, places, weights


def proximal(values, sums, places, weights):
    high = values + 0.5 * weights
    best = jnp.maximum(jnp.minimum(high, -1.0), values - 0.5 * weights)
    high = high + places
    for index in range(1, BINS):
        best = jnp.maximum(best, jnp.minimum(high - sums[index - 1], -1.0 + 2.0 * index / (BINS - 1)))
    return best


def block_of(index):
    half, column = index // 8, index % 8
    return half, column, pl.ds(pl.multiple_of(half * 8, 8), 8), pl.ds(pl.multiple_of(column * 128, 128), 128)


def slab_base():
    return (lax.axis_index("slab") * LAYERS).astype(jnp.float32)


def half_votes(half, caps_of, batches, tally):
    base = slab_base()
    caps = [caps_of[view] for view in range(VIEWS)]

    def body(column, carry):
        lanes = pl.ds(pl.multiple_of(column * 128, 128), 128)
        views = [ramps(batches[2 * view + half, column], base) for view in range(VIEWS)]
        for layer in range(LAYERS + 1):
            sums, places, weights = votes(views, caps, float(layer))
            for slot, total in enumerate(sums + [places, weights]):
                tally[slot, layer, :, lanes] = total
        return carry

    lax.fori_loop(0, 8, body, 0)


def low_votes(caps, batches, tally):
    half_votes(0, caps, batches, tally)


def high_votes(caps, batches, after, tally):
    half_votes(1, caps, batches, tally)


def joined(low, high, layer):
    return jnp.concatenate([low[layer], high[layer]], 0)


def second_votes(caps_of, batches, low, high, after, new_tally):
    base = slab_base()
    caps = [caps_of[VIEWS + view] for view in range(VIEWS)]
    for half, tally in ((0, low), (1, high)):

        def body(column, carry, half=half, tally=tally):
            lanes = pl.ds(pl.multiple_of(column * 128, 128), 128)
            views = [ramps(batches[2 * (VIEWS + view) + half, column], base) for view in range(VIEWS)]
            for layer in range(LAYERS):
                sums, places, weights = votes(views, caps, float(layer))
                for slot, total in enumerate(sums + [places, weights]):
                    new_tally[slot, layer, half * 8 : half * 8 + 8, lanes] = tally[slot, layer, :, lanes] + total
            return carry

        lax.fori_loop(0, 8, body, 0)


def counted(values, tally, layer):
    sums = [tally[slot, layer] for slot in range(BINS - 1)]
    return proximal(values, sums, tally[BINS - 1, layer], tally[BINS, layer])


def low_update(field, values, tally, updated, extra, side):
    for layer in range(LAYERS):
        new = counted(values[layer, 0:8, :], tally, layer)
        updated[layer] = new
        new = 2.0 * new - field[layer, 0:8, :]
        extra[layer] = new
        side[layer : layer + 1, :] = new[0:1, :]


def high_update(field, values, tally, updated, extra):
    for layer in range(LAYERS):
        new = counted(values[layer, 8:16, :], tally, layer)
        updated[layer] = new
        extra[layer] = 2.0 * new - field[layer, 8:16, :]


def past_update(below, values, dual, low, high, extra):
    for half, tally in ((0, low), (1, high)):
        rows = slice(half * 8, half * 8 + 8)
        steps = values[rows, :] - 0.25 * dual[0, LAYERS - 1, rows, :]
        extra[rows, :] = 2.0 * counted(steps, tally, LAYERS) - below[rows, :]


def top_dual(low, high, past, dual, ahead, top):
    last = LAYERS - 1
    slab_end = lax.axis_index("slab") == Z_LAST
    here, row = joined(low, high, last), ahead[last:LAYERS, :]
    top[...] = dual_layer(here, past[...], row, dual[0, last], dual[1, last], dual[2, last], slab_end)[0]


def last_layers(low, high, dual, before, tally, updated, part):
    part[...] = joined(low, high, 0) + 0.25 * (dual[0, 0] + flux_of(dual, before, 0))
    for layer in range(1, LAYERS):
        updated[layer] = counted(stepped(joined(low, high, layer), dual, None, before, layer), tally, layer)


def last_layer(part, above, tally, updated_in, updated, layer, sem):
    layer[...] = counted(part[...] - 0.25 * above[...], tally, 0)
    move = pltpu.make_async_copy(layer, updated.at[0], sem)
    move.start()
    move.wait()


def passed_along(value, axis, steps):
    count = lax.axis_size(axis)
    first, last = (max(0, -steps), min(count, count - steps))
    return lax.ppermute(value, axis, [(source, source + steps) for source in range(first, last)])


GROUPS = [[2 * place + half for place in range(16)] for half in range(2)]


def exchange(pieces):
    return lax.all_to_all(pieces, "slab", 0, 0, axis_index_groups=GROUPS)


def per_device(field, dual, depth, owner, visible):
    block = (LAYERS, ROWS, LANES)
    owner = pltpu.with_memory_space_constraint(owner, pltpu.HBM)
    visible = pltpu.with_memory_space_constraint(visible.transpose(0, 2, 1), pltpu.HBM)

    pieces = depth.reshape(16, 8, 8, 128).transpose(0, 2, 1, 3)
    spread = exchange(pieces)

    first_layer, first_rows, field, caps, mine = call(
        staged, [(ROWS, LANES), (LAYERS, LANES), block, (ITERS * VIEWS, 8, 128), (8, 128)], 1, [HBM] * 3,
        scratch_shapes=[
            pltpu.SMEM((ITERS,), jnp.int32), pltpu.SMEM((ITERS, 1, VIEWS), jnp.int32), pltpu.SemaphoreType.DMA((5,))
        ],
    )(owner, visible, pltpu.with_memory_space_constraint(field, pltpu.HBM))
    below = passed_along(first_layer, "slab", -1)
    (kept,) = call(pick, [(8, 8, 128)], 1, [SMEM, VMEM])(owner, spread)
    first_rows, _ = lax.optimization_barrier((first_rows, spread))
    ahead = passed_along(first_rows, "tile", -1)
    across = lax.ppermute(kept, "slab", [(index, index ^ 1) for index in range(32)])
    below, _ = lax.optimization_barrier((below, kept))
    (below,) = call(relay, [(ROWS, LANES)], 2, [VMEM])(below)
    layer, rows = (ROWS, LANES), (LAYERS, LANES)
    dual, top, side = call(all_duals, [(3,) + block, layer, rows], 1, [VMEM] * 4)(field, dual, ahead, below)
    above = passed_along(top, "slab", 1)
    before = passed_along(side, "tile", 1)
    across, top, side = lax.optimization_barrier((across, top, side))
    (copies,) = call(copies_of, [pieces.shape], 1, [VMEM] * 3)(mine, kept, across)
    batches = exchange(copies)
    (values,) = call(first_values, [layer], 1, [VMEM] * 3)(field, dual, before)
    past_values = passed_along(values, "slab", -1)
    (values,) = call(all_values, [block], 5, [VMEM] * 4)(field, dual, above, before)

    half, count = (LAYERS, 8, LANES), (BINS + 1, LAYERS + 1, 8, LANES)
    (low_tally,) = call(low_votes, [count], 12, [VMEM, VMEM])(caps, batches)
    low, low_extra, side = call(low_update, [half, half, rows], 1, [VMEM] * 3)(field, values, low_tally)
    ahead = passed_along(side, "tile", -1)
    (high_tally,) = call(high_votes, [count], 12, [VMEM, VMEM, ANY])(caps, batches, side)
    high, high_extra = call(high_update, [half, half], 1, [VMEM] * 3)(field, values, high_tally)
    past_values, _ = lax.optimization_barrier((past_values, high))
    (past,) = call(past_update, [layer], 1, [VMEM] * 5)(below, past_values, dual, low_tally, high_tally)
    (top,) = call(top_dual, [layer], 1, [VMEM] * 5)(low_extra, high_extra, past, dual, ahead)
    above = passed_along(top, "slab", 1)
    dual, side = call(second_duals, [(3,) + block, rows], 1, [VMEM] * 5 + [ANY])(
        low_extra, high_extra, dual, ahead, past, top
    )
    before = passed_along(side, "tile", 1)
    (tally,) = call(second_votes, [(BINS + 1,) + block], 3, [VMEM] * 4 + [ANY])(
        caps, batches, low_tally, high_tally, side
    )
    rest, part = call(last_layers, [block, layer], 1, [VMEM] * 5)(low, high, dual, before, tally)
    above, rest = lax.optimization_barrier((above, rest))
    (current,) = call(
        last_layer, [block], 1, [VMEM] * 3 + [ANY], out_specs=(ANY,), input_output_aliases={3: 0},
        scratch_shapes=[pltpu.VMEM((ROWS, LANES), jnp.float32), pltpu.SemaphoreType.DMA],
    )(part, above, tally, rest)
    return (current, dual)


def solution(mesh):
    placed = (
        P("slab", "tile", None),
        P(None, "slab", "tile", None),
        P("slab", None, None, "tile", None),
        P(),
        P(None, None, "tile"),
    )
    return jax.shard_map(
        per_device,
        mesh=mesh,
        in_specs=placed,
        out_specs=(P("slab", "tile", None), P(None, "slab", "tile", None)),
        check_vma=False,
    )
```
